256 devices in a mesh: blk: 16 (over y, x_lo, core), head: 16 (over x_hi, z).
Axes of the slice: x: 4 (x_hi: 2, x_lo: 2; x = x_hi * 2 + x_lo), y: 4, z: 8, core: 2. Of those that a mesh axis runs over, the one named last changes fastest.
Arguments:
- query: bfloat16 [8192, 8192], P(('blk', 'head')), may hold values from -6 to 6
- key: bfloat16 [8192, 1024], P(('blk', 'head')), may hold values from -6 to 6
- value: bfloat16 [8192, 1024], P(('blk', 'head')), may hold values from -6 to 6
- output: bfloat16 [8192, 8192], P(('blk', 'head')), may hold values from -1.5 to 1.5
- out_grad: bfloat16 [8192, 8192], P(('blk', 'head')), may hold values from -6 to 6
- lse: float32 [8192, 64], P(('blk', 'head')), may hold values from 3.5 to 6
- doc_lengths: int32 [7], replicated, may hold values from 1 to 2048, as said below
- block_keep: int32 [64, 17], P('blk'), may hold values 0 or 1
Outputs:
- query_grad: bfloat16 [8192, 8192], P(('blk', 'head'))
- key_grad: bfloat16 [8192, 1024], P(('blk', 'head'))
- value_grad: bfloat16 [8192, 1024], P(('blk', 'head'))
The draws below stay inside these ranges and needn't reach their ends.
Inputs may be any that keep to these rules, and one draw needn't show every extreme that they name: `doc_lengths`: whole document lengths that sum to 8192; the sequence is cut into aligned windows of 2048 tokens, each but the last split into two documents, the last one document of exactly 2048.
All inputs are finite; a program needn't handle non-finite values. No bound on the sum of `block_keep` on one device may be relied on, other than what follows from the above.
Results may differ from the reference program's by a relative error of at most 0.015.
Values may be sent and summed in bfloat16 or wider, within the bound.
No kernel may reach another device: no remote copies, remote signals or barrier semaphores. Data moves between devices by JAX's collectives and lax.ppermute only.
A program may use at most 128 MiB of HBM per device.

```python
import math
import jax
import jax.numpy as jnp
from jax import lax

HQ = 64
KVH = 8
HD = 128
TOK_BLK = 512
DOC_MAX = 2048
BLOCK = 128
TOKENS = 8192
NQB = 64
REACHB = 17


def draw_doc_lengths(key, part):
    windows = TOKENS // DOC_MAX
    cuts = jax.random.randint(key, (windows - 1,), 1, DOC_MAX, dtype=jnp.int32)
    pairs = jnp.stack([cuts, DOC_MAX - cuts], axis=1).reshape(-1)
    last = jnp.full((1,), DOC_MAX, jnp.int32)
    return jnp.concatenate([pairs, last]).astype(jnp.int32)


def set_ends(entries, rng, low, high):
    shape = entries.shape
    spot = [jax.random.randint(jax.random.fold_in(rng, axis), (), 0, shape[axis]) for axis in range(len(shape))]
    entries = entries.at[tuple(spot)].set(low)
    longest = shape.index(max(shape))
    spot[longest] = (spot[longest] + 1) % shape[longest]
    return entries.at[tuple(spot)].set(high)


def level_of(key, shape, shards, least, top_value):
    level, own = 1.0, jax.random.fold_in(key, 6)
    for position, shards_of in shards:
        draws = jnp.exp(jax.random.uniform(jax.random.fold_in(own, position), (shards_of,), jnp.float32, least / len(shards), top_value / len(shards)))
        level = level * jnp.repeat(draws, shape[position] // shards_of).reshape([-1 if axis == position else 1 for axis in range(len(shape))])
    return level


def centred(rng, shape, deviation, limit, cuts=(), held_as=jnp.bfloat16):
    factor_of = level_of(rng, shape, cuts, -0.22, 0.18) if cuts else 1.0
    array = jax.random.normal(rng, shape, jnp.float32) * deviation * factor_of
    return jnp.minimum(jnp.maximum(array, -limit), limit).astype(held_as)


def setup_inputs(seed: int = 0) -> dict:
    seeds = jax.random.split(jax.random.key(seed), 9)
    return {
        "query": centred(seeds[0], (TOKENS, HQ * HD), 1.0, 6.0, ((0, 256),)),
        "key": centred(seeds[1], (TOKENS, KVH * HD), 1.0, 6.0, ((0, 256),)),
        "value": centred(seeds[2], (TOKENS, KVH * HD), 1.0, 6.0, ((0, 256),)),
        "output": centred(seeds[3], (TOKENS, HQ * HD), 0.25, 1.5, ((0, 256),)),
        "out_grad": centred(seeds[4], (TOKENS, HQ * HD), 1.0, 6.0, ((0, 256),)),
        "lse": jnp.clip(3.5 + 2.5 * jax.random.uniform(seeds[5], (TOKENS, HQ), jnp.float32) ** level_of(seeds[5], (TOKENS, HQ), ((0, 256),), -0.2, 0.2), 3.5, 6.0),
        "doc_lengths": draw_doc_lengths(jax.random.fold_in(seeds[8], 71), 0),
        "block_keep": set_ends((jax.random.randint(seeds[7], (NQB, REACHB), 0, 4) < 3).astype(jnp.int32), jax.random.fold_in(seeds[7], 1), 0, 1),
    }


def doc_index(positions, starts):
    return lax.optimization_barrier(jnp.sum((positions[:, None] >= starts[None, :]).astype(jnp.int32), axis=1)) - 1

def block_table(first_query, first_key, rows, count_query, count_key):
    query_blocks = first_query // BLOCK + jnp.arange(count_query // BLOCK, dtype=jnp.int32)
    key_blocks = first_key // BLOCK + jnp.arange(count_key // BLOCK, dtype=jnp.int32)
    distance = query_blocks[:, None] - key_blocks[None, :]
    offsets = jnp.arange(rows.shape[1], dtype=jnp.int32)
    table = lax.optimization_barrier(jnp.sum(jnp.where(distance[:, :, None] == offsets[None, None, :], rows[:, None, :], 0), axis=2)) > 0
    return jnp.repeat(jnp.repeat(table, BLOCK, axis=0), BLOCK, axis=1)

def reference(query, key, value, output, out_grad, lse, doc_lengths, block_keep):
    f32 = jnp.float32
    group = HQ // KVH
    span = DOC_MAX + TOK_BLK
    scale = 1.0 / math.sqrt(HD)
    starts = (jnp.cumsum(doc_lengths) - doc_lengths).astype(jnp.int32)
    query4 = query.reshape(TOKENS, KVH, group, HD)
    grad4 = out_grad.reshape(TOKENS, KVH, group, HD)
    delta = lax.optimization_barrier(jnp.sum(grad4.astype(f32) * output.reshape(TOKENS, KVH, group, HD).astype(f32), axis=3))
    lse3 = lse.reshape(TOKENS, KVH, group)
    padding = jnp.zeros((DOC_MAX, KVH, HD), key.dtype)
    key_pad = jnp.concatenate([padding, key.reshape(TOKENS, KVH, HD)], axis=0)
    value_pad = jnp.concatenate([padding, value.reshape(TOKENS, KVH, HD)], axis=0)

    def one_head(parts):
        q_head, g_head, lse_head, delta_head, k_head, v_head = parts

        def tile(carry, index):
            dk_acc, dv_acc = carry
            first = (index * TOK_BLK).astype(jnp.int32)
            q_tile = lax.dynamic_slice_in_dim(q_head, first, TOK_BLK, 0).astype(f32)
            g_tile = lax.dynamic_slice_in_dim(g_head, first, TOK_BLK, 0).astype(f32)
            lse_tile = lax.dynamic_slice_in_dim(lse_head, first, TOK_BLK, 0)
            delta_tile = lax.dynamic_slice_in_dim(delta_head, first, TOK_BLK, 0)
            k_tile = lax.dynamic_slice_in_dim(k_head, first, span, 0).astype(f32)
            v_tile = lax.dynamic_slice_in_dim(v_head, first, span, 0).astype(f32)
            q_pos = first + jnp.arange(TOK_BLK, dtype=jnp.int32)
            k_pos = first - DOC_MAX + jnp.arange(span, dtype=jnp.int32)
            same = doc_index(q_pos, starts)[:, None] == doc_index(k_pos, starts)[None, :]
            causal = k_pos[None, :] <= q_pos[:, None]
            rows = lax.dynamic_slice_in_dim(block_keep, first // BLOCK, TOK_BLK // BLOCK, 0)
            allowed = same & causal & block_table(first, first - DOC_MAX, rows, TOK_BLK, span)
            scores = jnp.einsum('tgd,sd->gts', q_tile, k_tile) * scale
            probs = jnp.where(allowed[None], jnp.exp(scores - lse_tile.T[:, :, None]), 0.0)
            dprobs = jnp.einsum('tgd,sd->gts', g_tile, v_tile)
            dscores = probs * (dprobs - delta_tile.T[:, :, None])
            probs_b = lax.optimization_barrier(probs.astype(jnp.bfloat16)).astype(f32)
            dscores_b = lax.optimization_barrier(dscores.astype(jnp.bfloat16)).astype(f32)
            dv_part = jnp.einsum('gts,tgd->sd', probs_b, g_tile)
            dk_part = jnp.einsum('gts,tgd->sd', dscores_b, q_tile)
            dq_tile = (jnp.einsum('gts,sd->tgd', dscores_b, k_tile) * scale).astype(jnp.bfloat16)
            window_k = lax.dynamic_slice_in_dim(dk_acc, first, span, 0) + dk_part
            window_v = lax.dynamic_slice_in_dim(dv_acc, first, span, 0) + dv_part
            dk_acc = lax.dynamic_update_slice_in_dim(dk_acc, window_k, first, 0)
            dv_acc = lax.dynamic_update_slice_in_dim(dv_acc, window_v, first, 0)
            return ((dk_acc, dv_acc), dq_tile)
        zeros = jnp.zeros((TOKENS + DOC_MAX, HD), f32)
        (dk_acc, dv_acc), dq_tiles = lax.scan(tile, (zeros, zeros), jnp.arange(TOKENS // TOK_BLK, dtype=jnp.int32))
        dq_head = dq_tiles.reshape(TOKENS, group, HD)
        dk_head = (dk_acc[DOC_MAX:] * scale).astype(jnp.bfloat16)
        dv_head = dv_acc[DOC_MAX:].astype(jnp.bfloat16)
        return (dq_head, dk_head, dv_head)
    parts = (query4.transpose(1, 0, 2, 3), grad4.transpose(1, 0, 2, 3), lse3.transpose(1, 0, 2), delta.transpose(1, 0, 2), key_pad.transpose(1, 0, 2), value_pad.transpose(1, 0, 2))
    dq_all, dk_all, dv_all = lax.map(one_head, parts)
    query_grad = dq_all.transpose(1, 0, 2, 3).reshape(TOKENS, HQ * HD)
    key_grad = dk_all.transpose(1, 0, 2).reshape(TOKENS, KVH * HD)
    value_grad = dv_all.transpose(1, 0, 2).reshape(TOKENS, KVH * HD)
    return (query_grad, key_grad, value_grad)
```

```python
import math

import jax
import jax.numpy as jnp
from jax import lax
from jax.sharding import PartitionSpec as P

KVH = 8
HD = 128
DOC_MAX = 2048
BLOCK = 128


def from_behind(value, axis, by):
    length = lax.axis_size(axis)
    pairs = [(i, i + by) for i in range(length) if 0 <= i + by < length]
    return lax.ppermute(value, axis, pairs)


def passed_along(value, axis, by):
    length = lax.axis_size(axis)
    return lax.ppermute(value, axis, [(i, (i + by) % length) for i in range(length)])


def for_sending(value):
    return jax.tree.map(lambda a: a.astype(jnp.bfloat16) if a.dtype == jnp.float32 else a, value)


def doc_index(positions, starts):
    return jnp.sum((positions[:, None] >= starts[None, :]).astype(jnp.int32), axis=1) - 1


def block_table(first_query, first_key, rows, count_query, count_key):
    query_blocks = first_query // BLOCK + jnp.arange(count_query // BLOCK, dtype=jnp.int32)
    key_blocks = first_key // BLOCK + jnp.arange(count_key // BLOCK, dtype=jnp.int32)
    distance = query_blocks[:, None] - key_blocks[None, :]
    offsets = jnp.arange(rows.shape[1], dtype=jnp.int32)
    table = (
        jnp.sum(
            jnp.where(distance[:, :, None] == offsets[None, None, :], rows[:, None, :], 0), axis=2
        )
        > 0
    )
    return jnp.repeat(jnp.repeat(table, BLOCK, axis=0), BLOCK, axis=1)


def piece_grads(q_group, g_group, lse_group, delta_group, keys, values, allowed, scale):
    f32 = jnp.float32
    scores = jnp.einsum("tcgd,scd->cgts", q_group, keys, preferred_element_type=f32) * scale
    probs = jnp.where(allowed[None, None], jnp.exp(scores - lse_group[..., None]), 0.0)
    dprobs = jnp.einsum("tcgd,scd->cgts", g_group, values, preferred_element_type=f32)
    dscores = probs * (dprobs - delta_group[..., None])
    probs_b = probs.astype(jnp.bfloat16)
    dscores_b = dscores.astype(jnp.bfloat16)
    dv_part = jnp.einsum("cgts,tcgd->scd", probs_b, g_group, preferred_element_type=f32)
    dk_part = jnp.einsum("cgts,tcgd->scd", dscores_b, q_group, preferred_element_type=f32)
    dq_part = jnp.einsum("cgts,scd->tcgd", dscores_b, keys, preferred_element_type=f32)
    return (dq_part, dk_part, dv_part)


def shards(query, key, value, output, out_grad, lse, doc_lengths, block_keep):
    f32 = jnp.float32
    heads_axis = lax.axis_size("head")
    repeat = max(1, heads_axis // KVH)
    local_rows = query.shape[0]
    scale = 1.0 / math.sqrt(HD)
    q_range, o_range, g_range = (
        lax.all_to_all(query, "head", split_axis=1, concat_axis=0, tiled=True),
        lax.all_to_all(output, "head", split_axis=1, concat_axis=0, tiled=True),
        lax.all_to_all(out_grad, "head", split_axis=1, concat_axis=0, tiled=True),
    )
    lse_range = lax.all_to_all(lse, "head", split_axis=1, concat_axis=0, tiled=True)
    width = q_range.shape[1] // HD
    delta_range = jnp.sum(
        g_range.reshape(-1, width, HD).astype(f32) * o_range.reshape(-1, width, HD).astype(f32),
        axis=2,
    )
    key_rep = jnp.repeat(key.reshape(local_rows, KVH, HD), repeat, axis=1).reshape(
        local_rows, KVH * repeat * HD
    )
    value_rep = jnp.repeat(value.reshape(local_rows, KVH, HD), repeat, axis=1).reshape(
        local_rows, KVH * repeat * HD
    )
    key_range, value_range = (
        lax.all_to_all(key_rep, "head", split_axis=1, concat_axis=0, tiled=True),
        lax.all_to_all(value_rep, "head", split_axis=1, concat_axis=0, tiled=True),
    )
    range_rows = q_range.shape[0]
    local_heads = q_range.shape[1] // HD
    local_kv = key_range.shape[1] // HD
    group = local_heads // local_kv
    q_group = q_range.reshape(range_rows, local_kv, group, HD)
    g_group = g_range.reshape(range_rows, local_kv, group, HD)
    lse_group = lse_range.reshape(range_rows, local_kv, group).transpose(1, 2, 0)
    delta_group = delta_range.reshape(range_rows, local_kv, group).transpose(1, 2, 0)
    keys_own = key_range.reshape(range_rows, local_kv, HD)
    values_own = value_range.reshape(range_rows, local_kv, HD)
    documents = jnp.arange(doc_lengths.shape[0], dtype=jnp.int32)
    starts = jnp.sum(
        jnp.where(documents[None, :] < documents[:, None], doc_lengths[None, :], 0), axis=1
    )
    position = lax.axis_index("blk")
    first_query = position * range_rows
    q_pos = first_query + jnp.arange(range_rows, dtype=jnp.int32)
    q_doc = doc_index(q_pos, starts)

    def allowed_for(first_key):
        k_pos = first_key + jnp.arange(range_rows, dtype=jnp.int32)
        same = q_doc[:, None] == doc_index(k_pos, starts)[None, :]
        causal = k_pos[None, :] <= q_pos[:, None]
        return (
            same & causal & block_table(first_query, first_key, block_keep, range_rows, range_rows)
        )

    reach = DOC_MAX // range_rows
    half = range_rows // 2
    own_allowed = allowed_for(first_query)
    dq_upper, dk_upper, dv_upper = piece_grads(
        q_group[:half],
        g_group[:half],
        lse_group[..., :half],
        delta_group[..., :half],
        keys_own[:half],
        values_own[:half],
        own_allowed[:half, :half],
        scale,
    )
    dq_lower, dk_lower, dv_lower = piece_grads(
        q_group[half:],
        g_group[half:],
        lse_group[..., half:],
        delta_group[..., half:],
        keys_own,
        values_own,
        own_allowed[half:],
        scale,
    )
    dq_total = jnp.concatenate([dq_upper, dq_lower], axis=0)
    filler = jnp.zeros((range_rows - half,) + dk_upper.shape[1:], f32)
    dk_home = dk_lower + jnp.concatenate([dk_upper, filler], axis=0)
    dv_home = dv_lower + jnp.concatenate([dv_upper, filler], axis=0)
    moving = (keys_own, values_own)
    carried = (dk_home, dv_home)
    for step in range(1, reach + 1):
        moving = from_behind((moving[0], moving[1]), "blk", 1)
        carried = passed_along((carried[0], carried[1]), "blk", 1)
        dq_part, dk_part, dv_part = piece_grads(
            q_group,
            g_group,
            lse_group,
            delta_group,
            moving[0],
            moving[1],
            allowed_for((position - step) * range_rows),
            scale,
        )
        dq_total = dq_total + dq_part
        carried = (carried[0] + dk_part, carried[1] + dv_part)
    dk_final, dv_final = (
        passed_along(carried[0].astype(jnp.bfloat16), "blk", -reach).astype(jnp.float32),
        passed_along(carried[1].astype(jnp.bfloat16), "blk", -reach).astype(jnp.float32),
    )
    dk_rows = (dk_final * scale).reshape(range_rows, local_kv * HD)
    dv_rows = dv_final.reshape(range_rows, local_kv * HD)
    dk_back, dv_back = (
        lax.all_to_all(
            for_sending(dk_rows), "head", split_axis=0, concat_axis=1, tiled=True
        ).astype(dk_rows.dtype),
        lax.all_to_all(
            for_sending(dv_rows), "head", split_axis=0, concat_axis=1, tiled=True
        ).astype(dv_rows.dtype),
    )
    key_grad = jnp.sum(dk_back.reshape(local_rows, KVH, repeat, HD), axis=2).reshape(
        local_rows, KVH * HD
    )
    value_grad = jnp.sum(dv_back.reshape(local_rows, KVH, repeat, HD), axis=2).reshape(
        local_rows, KVH * HD
    )
    dq_rows = (dq_total * scale).astype(jnp.bfloat16).reshape(range_rows, local_heads * HD)
    query_grad = lax.all_to_all(dq_rows, "head", split_axis=0, concat_axis=1, tiled=True)
    return (query_grad, key_grad.astype(jnp.bfloat16), value_grad.astype(jnp.bfloat16))


def solution(mesh):
    in_specs = (
        P(("blk", "head"), None),
        P(("blk", "head"), None),
        P(("blk", "head"), None),
        P(("blk", "head"), None),
        P(("blk", "head"), None),
        P(("blk", "head"), None),
        P(),
        P("blk", None),
    )
    out_specs = (P(("blk", "head"), None), P(("blk", "head"), None), P(("blk", "head"), None))
    return jax.shard_map(shards, mesh=mesh, in_specs=in_specs, out_specs=out_specs, check_vma=False)
```

```python
import functools
import math

import jax
import jax.numpy as jnp
from jax import lax
from jax.experimental import pallas as pl
from jax.experimental.pallas import tpu as pltpu
from jax.sharding import Mesh
from jax.sharding import PartitionSpec as P

KVH = 8
HD = 128
GROUP = 8
BLOCK = 128
WINDOW = 2048
TOK = 32
ZS = 8
AS = 8
CHUNK = TOK * ZS
ROWS = TOK * GROUP
SCALE = 1.0 / math.sqrt(HD)
LOG2E = math.log2(math.e)
BIG = 1e30
HEADS = ("xl", "c", "xh")
F32 = jnp.float32
BF16 = jnp.bfloat16
OFFSETS = (0, 1, -1, 2, -2, 3, -3, 4)


def along_z(value, by):
    return lax.ppermute(value, "z", [(i, (i + by) % ZS) for i in range(ZS)])


def exchange(value):
    return lax.all_to_all(value, HEADS, split_axis=0, concat_axis=0, tiled=True)


def pack_kv_kernel(k_ref, v_ref, out_ref):
    for a in range(AS):
        out_ref[a, :, :HD] = k_ref[:, a * HD : (a + 1) * HD]
        out_ref[a, :, HD:] = v_ref[:, a * HD : (a + 1) * HD]


def pack_queries_kernel(q_ref, g_ref, extra_ref, out_ref):
    out_ref[0, :TOK, :] = q_ref[...]
    out_ref[0, TOK : 2 * TOK, :] = g_ref[...]
    out_ref[0, 2 * TOK :, :ROWS] = extra_ref[0]
    out_ref[0, 2 * TOK :, ROWS:] = jnp.zeros((16, GROUP * HD - ROWS), BF16)


def attention_kernel(keep_ref, span_ref, z_ref, message_ref, start_ref, *refs):
    kv_refs, refs = refs[:ZS], refs[ZS:]
    dq_ref, refs = refs[0], refs[1:]
    dkv_refs, refs = refs[:ZS], refs[ZS:]
    acc_ref, kt_ref, q_ref, g_ref, qt_ref, gt_ref, dqt_ref = refs
    z = z_ref[0]
    sources = [lax.rem(z - off + ZS, ZS) for off in OFFSETS]

    def keys_of(a, lanes):
        return jnp.concatenate([kv[a, :, lanes] for kv in kv_refs], axis=0)

    def prepare(a, _):
        kt_ref[a] = keys_of(a, pl.ds(0, HD)).T
        acc_ref[a] = jnp.zeros((CHUNK, 2 * HD), F32)
        return 0

    lax.fori_loop(0, AS, prepare, 0)

    def chunk(i, _):
        for h in range(GROUP):
            q_ref[h * TOK : (h + 1) * TOK, :] = message_ref[i, :TOK, h * HD : (h + 1) * HD]
            g_ref[h * TOK : (h + 1) * TOK, :] = message_ref[i, TOK : 2 * TOK, h * HD : (h + 1) * HD]
        qt_ref[...] = q_ref[...].T
        gt_ref[...] = g_ref[...].T
        extra = message_ref[i, 2 * TOK :, :ROWS].astype(F32)
        lse = extra[0:1] + extra[1:2]
        delta = extra[2:3] + extra[3:4]
        start = start_ref[i]
        q_pos = i * CHUNK + z * TOK + lax.rem(lax.broadcasted_iota(jnp.int32, (1, ROWS), 1), TOK)
        dqt_ref[...] = jnp.zeros((HD, ROWS), F32)

        def tile(a, masked):
            scores = jnp.dot(keys_of(a, pl.ds(0, HD)), qt_ref[...], preferred_element_type=F32)
            dprobs = jnp.dot(keys_of(a, pl.ds(HD, HD)), gt_ref[...], preferred_element_type=F32)
            probs_b, dscores_b = [], []
            for r in range(ZS):
                rows = slice(r * TOK, (r + 1) * TOK)
                distance = 2 * (i - a) + z // 4 - sources[r] // 4
                kept = keep_ref[i, jnp.maximum(distance, 0)] > 0
                lse_piece = lse + jnp.where(kept, 0.0, BIG)
                probs = jnp.exp2(scores[rows] * (SCALE * LOG2E) - lse_piece)
                if masked:
                    k_pos = (
                        a * CHUNK
                        + sources[r] * TOK
                        + lax.broadcasted_iota(jnp.int32, (TOK, ROWS), 0)
                    )
                    probs = jnp.where((k_pos >= start) & (k_pos <= q_pos), probs, 0.0)
                probs_b.append(probs.astype(BF16))
                dscores_b.append((probs * (dprobs[rows] - delta)).astype(BF16))
            probs_b = jnp.concatenate(probs_b, axis=0)
            dscores_b = jnp.concatenate(dscores_b, axis=0)
            acc_ref[a, :, :HD] += jnp.dot(dscores_b, q_ref[...], preferred_element_type=F32)
            acc_ref[a, :, HD:] += jnp.dot(probs_b, g_ref[...], preferred_element_type=F32)
            dqt_ref[...] += jnp.dot(kt_ref[a], dscores_b, preferred_element_type=F32)

        def step(a, _):
            masked = (a == i) | (span_ref[i, 1] > a * CHUNK)

            @pl.when(masked)
            def _():
                tile(a, True)

            @pl.when(jnp.logical_not(masked))
            def _():
                tile(a, False)

            return 0

        lax.fori_loop(span_ref[i, 0] // CHUNK, i + 1, step, 0)
        dq = (dqt_ref[...] * SCALE).T.astype(BF16)
        for h in range(GROUP):
            dq_ref[i, :, h * HD : (h + 1) * HD] = dq[h * TOK : (h + 1) * TOK]
        return 0

    lax.fori_loop(0, AS, chunk, 0)

    def finish(a, _):
        for r in range(ZS):
            piece = acc_ref[a, r * TOK : (r + 1) * TOK, :]
            dkv_refs[r][a, :, :HD] = (piece[:, :HD] * SCALE).astype(BF16)
            dkv_refs[r][a, :, HD:] = piece[:, HD:].astype(BF16)
        return 0

    lax.fori_loop(0, AS, finish, 0)


def sum_kernel(*refs):
    total = refs[0][...].astype(F32)
    for ref in refs[1:-1]:
        total = total + ref[...].astype(F32)
    refs[-1][...] = total.astype(BF16)


def unpack_queries_kernel(in_ref, out_ref):
    out_ref[...] = in_ref[0]


def unpack_kv_kernel(in_ref, dk_ref, dv_ref):
    for a in range(AS):
        dk_ref[:, a * HD : (a + 1) * HD] = in_ref[a, :, :HD]
        dv_ref[:, a * HD : (a + 1) * HD] = in_ref[a, :, HD:]


def in_vmem():
    return pl.BlockSpec(memory_space=pltpu.VMEM)


def in_smem():
    return pl.BlockSpec(memory_space=pltpu.SMEM)


def shards(query, key, value, output, out_grad, lse, doc_lengths, block_keep):
    i32 = jnp.int32
    z = lax.axis_index("z").astype(i32)
    columns = GROUP * HD

    kv_send = pl.pallas_call(
        pack_kv_kernel,
        out_shape=jax.ShapeDtypeStruct((AS, TOK, 2 * HD), BF16),
        in_specs=[in_vmem(), in_vmem()],
        out_specs=in_vmem(),
        cost_estimate=pl.CostEstimate(flops=0, bytes_accessed=262144, transcendentals=0),
    )(key, value)
    kv_own = exchange(kv_send)

    delta = jnp.sum(
        out_grad.reshape(TOK, -1, HD).astype(F32) * output.reshape(TOK, -1, HD).astype(F32), axis=2
    )
    both = jnp.stack([lse * LOG2E, delta])
    high = lax.reduce_precision(both, 8, 7)
    parts = jnp.stack([high, both - high], axis=1).astype(BF16)
    parts = parts.reshape(4, TOK, AS, GROUP).transpose(2, 0, 3, 1).reshape(AS, 4, ROWS)
    local_block = lax.axis_index("xh") * 2 + z // 4
    keep_row = lax.dynamic_slice_in_dim(block_keep, local_block, 1, 0).astype(BF16)
    reach = keep_row.shape[1]
    keep_row = jnp.broadcast_to(jnp.pad(keep_row, ((0, 0), (0, ROWS - reach)))[None], (AS, 1, ROWS))
    extra = jnp.concatenate([parts, keep_row, jnp.zeros((AS, 11, ROWS), BF16)], axis=1)
    message_send = pl.pallas_call(
        pack_queries_kernel,
        grid=(AS,),
        out_shape=jax.ShapeDtypeStruct((AS, 2 * TOK + 16, columns), BF16),
        in_specs=[
            pl.BlockSpec((TOK, columns), lambda a: (0, a)),
            pl.BlockSpec((TOK, columns), lambda a: (0, a)),
            pl.BlockSpec((1, 16, ROWS), lambda a: (a, 0, 0)),
        ],
        out_specs=pl.BlockSpec((1, 2 * TOK + 16, columns), lambda a: (a, 0, 0)),
        cost_estimate=pl.CostEstimate(flops=0, bytes_accessed=2600000, transcendentals=0),
    )(query, out_grad, extra)
    message = exchange(message_send)

    pieces = {0: kv_own}
    for off in (1, 2, 3, 4):
        pieces[off] = along_z(pieces[off - 1], 1)
        if off < 4:
            pieces[-off] = along_z(pieces[1 - off], -1)

    keep = message[:, 2 * TOK + 4, :reach].astype(i32)
    ends = jnp.arange(doc_lengths.shape[0], dtype=i32)
    starts = jnp.sum(jnp.where(ends[None, :] < ends[:, None], doc_lengths[None, :], 0), axis=1)
    base = lax.axis_index("y").astype(i32) * WINDOW
    positions = (
        base
        + jnp.arange(AS, dtype=i32)[:, None] * CHUNK
        + z * TOK
        + (jnp.arange(ROWS, dtype=i32) % TOK)[None, :]
    )
    start_of = jnp.max(
        jnp.where(starts[None, None, :] <= positions[:, :, None], starts[None, None, :], 0), axis=2
    )
    start_of = jnp.maximum(start_of - base, 0)
    span = jnp.stack([start_of[:, 0], start_of[:, TOK - 1]], axis=1)

    piece_shape = jax.ShapeDtypeStruct((AS, TOK, 2 * HD), BF16)
    results = pl.pallas_call(
        attention_kernel,
        out_shape=[jax.ShapeDtypeStruct((AS, TOK, columns), BF16)] + [piece_shape] * ZS,
        in_specs=[in_smem()] * 3 + [in_vmem()] * (2 + ZS),
        out_specs=[in_vmem()] * (1 + ZS),
        scratch_shapes=[
            pltpu.VMEM((AS, CHUNK, 2 * HD), F32),
            pltpu.VMEM((AS, HD, CHUNK), BF16),
            pltpu.VMEM((ROWS, HD), BF16),
            pltpu.VMEM((ROWS, HD), BF16),
            pltpu.VMEM((HD, ROWS), BF16),
            pltpu.VMEM((HD, ROWS), BF16),
            pltpu.VMEM((HD, ROWS), F32),
        ],
        compiler_params=pltpu.CompilerParams(vmem_limit_bytes=24 * 2**20),
        cost_estimate=pl.CostEstimate(
            flops=3000000000, bytes_accessed=4000000, transcendentals=2360000
        ),
    )(keep, span, z.reshape(1), message, start_of.reshape(AS, 1, ROWS), *[pieces[o] for o in OFFSETS])
    dq, partials = results[0], results[1:]

    returned = [
        partials[r] if off == 0 else along_z(partials[r], -off) for r, off in enumerate(OFFSETS)
    ]
    dq_back = exchange(dq)
    query_grad = pl.pallas_call(
        unpack_queries_kernel,
        grid=(AS,),
        out_shape=jax.ShapeDtypeStruct((TOK, AS * columns), BF16),
        in_specs=[pl.BlockSpec((1, TOK, columns), lambda a: (a, 0, 0))],
        out_specs=pl.BlockSpec((TOK, columns), lambda a: (0, a)),
        cost_estimate=pl.CostEstimate(flops=0, bytes_accessed=1048576, transcendentals=0),
    )(dq_back)
    summed = pl.pallas_call(
        sum_kernel,
        out_shape=piece_shape,
        in_specs=[in_vmem()] * ZS,
        out_specs=in_vmem(),
        cost_estimate=pl.CostEstimate(flops=524288, bytes_accessed=1179648, transcendentals=0),
    )(*returned)
    grads = exchange(summed)
    half = jax.ShapeDtypeStruct((TOK, KVH * HD), BF16)
    key_grad, value_grad = pl.pallas_call(
        unpack_kv_kernel,
        out_shape=[half, half],
        in_specs=[in_vmem()],
        out_specs=[in_vmem(), in_vmem()],
        cost_estimate=pl.CostEstimate(flops=0, bytes_accessed=262144, transcendentals=0),
    )(grads)
    return (query_grad, key_grad, value_grad)


def solution(mesh):
    fine = Mesh(mesh.devices.reshape(4, 2, 2, 2, ZS), ("y", "xl", "c", "xh", "z"))
    tokens = P(("y", "xl", "c", "xh", "z"), None)
    in_specs = (tokens,) * 6 + (P(), P(("y", "xl", "c"), None))
    return jax.shard_map(
        shards, mesh=fine, in_specs=in_specs, out_specs=(tokens,) * 3, check_vma=False
    )
```

```python
import functools
import math

import jax
import jax.numpy as jnp
from jax import lax
from jax.experimental import pallas as pl
from jax.experimental.pallas import tpu as pltpu
from jax.sharding import Mesh
from jax.sharding import PartitionSpec as P

KVH = 8
HD = 128
GROUP = 8
BLOCK = 128
WINDOW = 2048
TOK = 32
ZS = 8
AS = 8
CHUNK = TOK * ZS
ROWS = TOK * GROUP
SCALE = 1.0 / math.sqrt(HD)
LOG2E = math.log2(math.e)
BIG = 1e30
EXTRA = 8
HEADS = ("xl", "c", "xh")
F32 = jnp.float32
BF16 = jnp.bfloat16
OFFSETS = (0, 1, -1, 2, -2, 3, -3, 4)


def along_z(value, by):
    return lax.ppermute(value, "z", [(i, (i + by) % ZS) for i in range(ZS)])


def exchange(value):
    return lax.all_to_all(value, HEADS, split_axis=0, concat_axis=0, tiled=True)


def pack_kv_kernel(k_ref, v_ref, out_ref):
    for a in range(AS):
        out_ref[a, :, :HD] = k_ref[:, a * HD : (a + 1) * HD]
        out_ref[a, :, HD:] = v_ref[:, a * HD : (a + 1) * HD]


def split(value):
    high = value.astype(BF16)
    return high, (value - high.astype(F32)).astype(BF16)


def pack_queries_kernel(place_ref, keep_ref, q_ref, g_ref, o_ref, lse_ref, out_ref):
    ones = jnp.ones((EXTRA, 2 * HD), BF16)
    lane = lax.broadcasted_iota(jnp.int32, (TOK, ROWS), 1)
    spread = (lane % TOK == lax.broadcasted_iota(jnp.int32, (TOK, ROWS), 0)).astype(F32).astype(BF16)
    head_lane = lax.broadcasted_iota(jnp.int32, (GROUP, ROWS), 1) // TOK
    own_head = head_lane == lax.broadcasted_iota(jnp.int32, (GROUP, ROWS), 0)
    row = lax.broadcasted_iota(jnp.int32, (EXTRA, ROWS), 0)
    flag_lane = lax.broadcasted_iota(jnp.int32, (1, ROWS), 1)
    flags = jnp.zeros((1, ROWS), F32)
    for d in range(keep_ref.shape[1]):
        flags = jnp.where(flag_lane == d, keep_ref[place_ref[0], d].astype(F32), flags)
    high, low = split(lse_ref[...])
    low, lower = low, split(lse_ref[...] - high.astype(F32) - low.astype(F32))[0]
    lse_all = sum(jnp.dot(p, spread, preferred_element_type=F32) for p in (high, low, lower))
    for a in range(AS):
        columns = slice(a * GROUP * HD, (a + 1) * GROUP * HD)
        q_block, g_block = q_ref[:, columns], g_ref[:, columns]
        out_ref[a, :TOK, :] = q_block
        out_ref[a, TOK : 2 * TOK, :] = g_block
        product = g_block.astype(F32) * o_ref[:, columns].astype(F32)
        high, low = split(product)
        stacked = jnp.concatenate(
            [
                jnp.concatenate([p[:, h * HD : (h + 1) * HD] for h in range(GROUP)], axis=0)
                for p in (high, low)
            ],
            axis=1,
        )
        delta = lax.dot_general(
            ones, stacked, (((1,), (1,)), ((), ())), preferred_element_type=F32
        )[:1]
        lse = jnp.sum(
            jnp.where(own_head, lse_all[a * GROUP : (a + 1) * GROUP], 0.0), axis=0, keepdims=True
        )
        lse_high, lse_low = split(lse)
        delta_high, delta_low = split(delta)
        extra = jnp.zeros((EXTRA, ROWS), F32)
        for n, part in enumerate((lse_high, lse_low, delta_high, delta_low, flags)):
            extra = jnp.where(row == n, part.astype(F32), extra)
        out_ref[a, 2 * TOK :, :ROWS] = extra.astype(BF16)
        out_ref[a, 2 * TOK :, ROWS:] = jnp.zeros((EXTRA, GROUP * HD - ROWS), BF16)


def attention_kernel(keep_ref, span_ref, z_ref, message_ref, start_ref, *refs):
    kv_refs, refs = refs[:ZS], refs[ZS:]
    dq_ref, refs = refs[0], refs[1:]
    dkv_refs, refs = refs[:ZS], refs[ZS:]
    acc_ref, kt_ref, q_ref, g_ref, qt_ref, gt_ref, dqt_ref = refs
    z = z_ref[0]
    sources = [lax.rem(z - off + ZS, ZS) for off in OFFSETS]

    def keys_of(a, lanes):
        return jnp.concatenate([kv[a, :, lanes] for kv in kv_refs], axis=0)

    def prepare(a, _):
        kt_ref[a] = keys_of(a, pl.ds(0, HD)).T
        acc_ref[a] = jnp.zeros((CHUNK, 2 * HD), F32)
        return 0

    lax.fori_loop(0, AS, prepare, 0)

    def chunk(i, _):
        for h in range(GROUP):
            q_ref[h * TOK : (h + 1) * TOK, :] = message_ref[i, :TOK, h * HD : (h + 1) * HD]
            g_ref[h * TOK : (h + 1) * TOK, :] = message_ref[i, TOK : 2 * TOK, h * HD : (h + 1) * HD]
        qt_ref[...] = q_ref[...].T
        gt_ref[...] = g_ref[...].T
        extra = message_ref[i, 2 * TOK :, :ROWS].astype(F32)
        lse = extra[0:1] + extra[1:2]
        delta = extra[2:3] + extra[3:4]
        start = start_ref[i]
        q_pos = i * CHUNK + z * TOK + lax.rem(lax.broadcasted_iota(jnp.int32, (1, ROWS), 1), TOK)
        dqt_ref[...] = jnp.zeros((HD, ROWS), F32)

        def tile(a, masked):
            scores = jnp.dot(keys_of(a, pl.ds(0, HD)), qt_ref[...], preferred_element_type=F32)
            dprobs = jnp.dot(keys_of(a, pl.ds(HD, HD)), gt_ref[...], preferred_element_type=F32)
            probs_b, dscores_b = [], []
            for r in range(ZS):
                rows = slice(r * TOK, (r + 1) * TOK)
                distance = 2 * (i - a) + z // 4 - sources[r] // 4
                kept = keep_ref[i, jnp.maximum(distance, 0)] > 0
                lse_piece = lse + jnp.where(kept, 0.0, BIG)
                probs = jnp.exp2(scores[rows] * (SCALE * LOG2E) - lse_piece)
                if masked:
                    k_pos = (
                        a * CHUNK
                        + sources[r] * TOK
                        + lax.broadcasted_iota(jnp.int32, (TOK, ROWS), 0)
                    )
                    probs = jnp.where((k_pos >= start) & (k_pos <= q_pos), probs, 0.0)
                probs_b.append(probs.astype(BF16))
                dscores_b.append((probs * (dprobs[rows] - delta)).astype(BF16))
            probs_b = jnp.concatenate(probs_b, axis=0)
            dscores_b = jnp.concatenate(dscores_b, axis=0)
            acc_ref[a, :, :HD] += jnp.dot(dscores_b, q_ref[...], preferred_element_type=F32)
            acc_ref[a, :, HD:] += jnp.dot(probs_b, g_ref[...], preferred_element_type=F32)
            dqt_ref[...] += jnp.dot(kt_ref[a], dscores_b, preferred_element_type=F32)

        def step(a, _):
            masked = (a == i) | (span_ref[i, 1] > a * CHUNK)

            @pl.when(masked)
            def _():
                tile(a, True)

            @pl.when(jnp.logical_not(masked))
            def _():
                tile(a, False)

            return 0

        lax.fori_loop(span_ref[i, 0] // CHUNK, i + 1, step, 0)
        dq = (dqt_ref[...] * SCALE).T.astype(BF16)
        for h in range(GROUP):
            dq_ref[i, :, h * HD : (h + 1) * HD] = dq[h * TOK : (h + 1) * TOK]
        return 0

    lax.fori_loop(0, AS, chunk, 0)

    def finish(a, _):
        for r in range(ZS):
            piece = acc_ref[a, r * TOK : (r + 1) * TOK, :]
            dkv_refs[r][a, :, :HD] = (piece[:, :HD] * SCALE).astype(BF16)
            dkv_refs[r][a, :, HD:] = piece[:, HD:].astype(BF16)
        return 0

    lax.fori_loop(0, AS, finish, 0)


def sum_kernel(*refs):
    total = refs[0][...].astype(F32)
    for ref in refs[1:-1]:
        total = total + ref[...].astype(F32)
    refs[-1][...] = total.astype(BF16)


def unpack_queries_kernel(in_ref, out_ref):
    for a in range(AS):
        out_ref[:, a * GROUP * HD : (a + 1) * GROUP * HD] = in_ref[a]


def unpack_kv_kernel(in_ref, dk_ref, dv_ref):
    for a in range(AS):
        dk_ref[:, a * HD : (a + 1) * HD] = in_ref[a, :, :HD]
        dv_ref[:, a * HD : (a + 1) * HD] = in_ref[a, :, HD:]


def in_vmem():
    return pl.BlockSpec(memory_space=pltpu.VMEM)


def in_smem():
    return pl.BlockSpec(memory_space=pltpu.SMEM)


def shards(query, key, value, output, out_grad, lse, doc_lengths, block_keep):
    i32 = jnp.int32
    z = lax.axis_index("z").astype(i32)
    columns = GROUP * HD

    kv_send = pl.pallas_call(
        pack_kv_kernel,
        out_shape=jax.ShapeDtypeStruct((AS, TOK, 2 * HD), BF16),
        in_specs=[in_vmem(), in_vmem()],
        out_specs=in_vmem(),
        compiler_params=pltpu.CompilerParams(vmem_limit_bytes=4 * 2**20),
        cost_estimate=pl.CostEstimate(flops=0, bytes_accessed=262144, transcendentals=0),
    )(key, value)
    kv_own = exchange(kv_send)

    place = (lax.axis_index("xh") * 2 + z // 4).astype(i32).reshape(1)
    reach = block_keep.shape[1]
    message_send = pl.pallas_call(
        pack_queries_kernel,
        out_shape=jax.ShapeDtypeStruct((AS, 2 * TOK + EXTRA, columns), BF16),
        in_specs=[in_smem(), in_smem()] + [in_vmem()] * 4,
        out_specs=in_vmem(),
        compiler_params=pltpu.CompilerParams(vmem_limit_bytes=16 * 2**20),
        cost_estimate=pl.CostEstimate(flops=67108864, bytes_accessed=2800000, transcendentals=0),
    )(place, block_keep, query, out_grad, output, lse.T * LOG2E)
    message = exchange(message_send)

    pieces = {0: kv_own}
    for off in (1, 2, 3, 4):
        pieces[off] = along_z(pieces[off - 1], 1)
        if off < 4:
            pieces[-off] = along_z(pieces[1 - off], -1)

    keep = message[:, 2 * TOK + 4, :reach].astype(i32)
    ends = jnp.arange(doc_lengths.shape[0], dtype=i32)
    starts = jnp.sum(jnp.where(ends[None, :] < ends[:, None], doc_lengths[None, :], 0), axis=1)
    base = lax.axis_index("y").astype(i32) * WINDOW
    positions = (
        base
        + jnp.arange(AS, dtype=i32)[:, None] * CHUNK
        + z * TOK
        + (jnp.arange(ROWS, dtype=i32) % TOK)[None, :]
    )
    start_of = jnp.max(
        jnp.where(starts[None, None, :] <= positions[:, :, None], starts[None, None, :], 0), axis=2
    )
    start_of = jnp.maximum(start_of - base, 0)
    span = jnp.stack([start_of[:, 0], start_of[:, TOK - 1]], axis=1)

    piece_shape = jax.ShapeDtypeStruct((AS, TOK, 2 * HD), BF16)
    results = pl.pallas_call(
        attention_kernel,
        out_shape=[jax.ShapeDtypeStruct((AS, TOK, columns), BF16)] + [piece_shape] * ZS,
        in_specs=[in_smem()] * 3 + [in_vmem()] * (2 + ZS),
        out_specs=[in_vmem()] * (1 + ZS),
        scratch_shapes=[
            pltpu.VMEM((AS, CHUNK, 2 * HD), F32),
            pltpu.VMEM((AS, HD, CHUNK), BF16),
            pltpu.VMEM((ROWS, HD), BF16),
            pltpu.VMEM((ROWS, HD), BF16),
            pltpu.VMEM((HD, ROWS), BF16),
            pltpu.VMEM((HD, ROWS), BF16),
            pltpu.VMEM((HD, ROWS), F32),
        ],
        compiler_params=pltpu.CompilerParams(vmem_limit_bytes=24 * 2**20),
        cost_estimate=pl.CostEstimate(
            flops=3000000000, bytes_accessed=4000000, transcendentals=2360000
        ),
    )(keep, span, z.reshape(1), message, start_of.reshape(AS, 1, ROWS), *[pieces[o] for o in OFFSETS])
    dq, partials = results[0], results[1:]

    returned = [
        partials[r] if off == 0 else along_z(partials[r], -off) for r, off in enumerate(OFFSETS)
    ]
    dq_back = exchange(dq)
    returned, dq_back = lax.optimization_barrier((returned, dq_back))
    query_grad = pl.pallas_call(
        unpack_queries_kernel,
        out_shape=jax.ShapeDtypeStruct((TOK, AS * columns), BF16),
        in_specs=[in_vmem()],
        out_specs=in_vmem(),
        compiler_params=pltpu.CompilerParams(vmem_limit_bytes=4 * 2**20),
        cost_estimate=pl.CostEstimate(flops=0, bytes_accessed=1048576, transcendentals=0),
    )(dq_back)
    summed = pl.pallas_call(
        sum_kernel,
        out_shape=piece_shape,
        in_specs=[in_vmem()] * ZS,
        out_specs=in_vmem(),
        compiler_params=pltpu.CompilerParams(vmem_limit_bytes=4 * 2**20),
        cost_estimate=pl.CostEstimate(flops=524288, bytes_accessed=1179648, transcendentals=0),
    )(*returned)
    grads = exchange(summed)
    half = jax.ShapeDtypeStruct((TOK, KVH * HD), BF16)
    key_grad, value_grad = pl.pallas_call(
        unpack_kv_kernel,
        out_shape=[half, half],
        in_specs=[in_vmem()],
        out_specs=[in_vmem(), in_vmem()],
        compiler_params=pltpu.CompilerParams(vmem_limit_bytes=4 * 2**20),
        cost_estimate=pl.CostEstimate(flops=0, bytes_accessed=262144, transcendentals=0),
    )(grads)
    return (query_grad, key_grad, value_grad)


def solution(mesh):
    fine = Mesh(mesh.devices.reshape(4, 2, 2, 2, ZS), ("y", "xl", "c", "xh", "z"))
    tokens = P(("y", "xl", "c", "xh", "z"), None)
    in_specs = (tokens,) * 6 + (P(), P(("y", "xl", "c"), None))
    return jax.shard_map(
        shards, mesh=fine, in_specs=in_specs, out_specs=(tokens,) * 3, check_vma=False
    )
```

```python
import math

import jax
import jax.numpy as jnp
from jax import lax
from jax.experimental import pallas as pl
from jax.experimental.pallas import tpu as pltpu
from jax.sharding import Mesh
from jax.sharding import PartitionSpec as P

KVH = 8
HD = 128
GROUP = 8
BLOCK = 128
WINDOW = 2048
TOK = 32
ZS = 8
AS = 8
CHUNK = TOK * ZS
ROWS = TOK * GROUP
SCALE = 1.0 / math.sqrt(HD)
LOG2E = math.log2(math.e)
BIG = 1e30
PAIR = 2
EXTRA = 8
HEADS = ("xl", "c", "xh")
F32 = jnp.float32
BF16 = jnp.bfloat16
OFFSETS = (0, 1, -1, 2, -2, 3, -3, 4)


def along_z(value, by):
    return lax.ppermute(value, "z", [(i, (i + by) % ZS) for i in range(ZS)])


def exchange(value):
    return lax.all_to_all(value, HEADS, split_axis=0, concat_axis=0, tiled=True)


def run_copies(copies):
    for copy in copies:
        copy.start()
    for copy in copies:
        copy.wait()


def pack_kv_kernel(k_ref, v_ref, out_ref, sems):
    run_copies(
        [
            pltpu.make_async_copy(
                ref.at[:, pl.ds(a * HD, HD)], out_ref.at[a, :, pl.ds(n * HD, HD)], sems.at[n, a]
            )
            for n, ref in enumerate((k_ref, v_ref))
            for a in range(AS)
        ]
    )


def split(value):
    high = value.astype(BF16)
    return high, (value - high.astype(F32)).astype(BF16)


def pack_queries_kernel(
    q_hbm, g_hbm, o_hbm, lse_hbm, keep_hbm, out_ref, o_ref, lse_ref, keep_ref, row_ref, sems, small
):
    wide = GROUP * HD
    copies = [[], []]
    small_copies = [
        pltpu.make_async_copy(lse_hbm, lse_ref, small.at[0]),
        pltpu.make_async_copy(keep_hbm, keep_ref, small.at[1]),
    ]
    for copy in small_copies:
        copy.start()
    for a in range(AS):
        columns = pl.ds(a * wide, wide)
        for n, (src, dst) in enumerate(
            (
                (g_hbm, out_ref.at[a, pl.ds(TOK, TOK), :]),
                (o_hbm, o_ref.at[:, columns]),
            )
        ):
            copies[0].append(pltpu.make_async_copy(src.at[:, columns], dst, sems.at[n, a]))
        copies[1].append(
            pltpu.make_async_copy(
                q_hbm.at[:, columns], out_ref.at[a, pl.ds(0, TOK), :], sems.at[2, a]
            )
        )
    for copy in copies[0] + copies[1]:
        copy.start()
    ones = jnp.ones((EXTRA, 2 * HD), BF16)
    lane = lax.broadcasted_iota(jnp.int32, (TOK, ROWS), 1)
    spread = (lane % TOK == lax.broadcasted_iota(jnp.int32, (TOK, ROWS), 0)).astype(F32).astype(BF16)
    head_lane = lax.broadcasted_iota(jnp.int32, (GROUP, ROWS), 1) // TOK
    own_head = head_lane == lax.broadcasted_iota(jnp.int32, (GROUP, ROWS), 0)
    row = lax.broadcasted_iota(jnp.int32, (EXTRA, ROWS), 0)
    for copy in small_copies:
        copy.wait()
    place = lax.axis_index("xh") * 2 + lax.axis_index("z") // 4
    kept = keep_ref[...].astype(F32)
    at_place = lax.broadcasted_iota(jnp.int32, kept.shape, 0) == place
    row_ref[...] = jnp.zeros(row_ref.shape, F32)
    row_ref[0:1, : kept.shape[1]] = jnp.sum(jnp.where(at_place, kept, 0.0), axis=0, keepdims=True)
    flags = row_ref[0:1]
    scaled = lse_ref[...].T * LOG2E
    high, low = split(scaled)
    lower = split(scaled - high.astype(F32) - low.astype(F32))[0]
    lse_all = sum(jnp.dot(p, spread, preferred_element_type=F32) for p in (high, low, lower))
    for a in range(AS):
        copies[0][2 * a].wait()
        copies[0][2 * a + 1].wait()
        columns = slice(a * wide, (a + 1) * wide)
        product = out_ref[a, TOK : 2 * TOK, :].astype(F32) * o_ref[:, columns].astype(F32)
        high, low = split(product)
        stacked = jnp.concatenate(
            [
                jnp.concatenate([p[:, h * HD : (h + 1) * HD] for h in range(GROUP)], axis=0)
                for p in (high, low)
            ],
            axis=1,
        )
        delta = lax.dot_general(
            ones, stacked, (((1,), (1,)), ((), ())), preferred_element_type=F32
        )[:1]
        lse = jnp.sum(
            jnp.where(own_head, lse_all[a * GROUP : (a + 1) * GROUP], 0.0), axis=0, keepdims=True
        )
        lse_high, lse_low = split(lse)
        delta_high, delta_low = split(delta)
        extra = jnp.zeros((EXTRA, ROWS), F32)
        for n, part in enumerate((lse_high, lse_low, delta_high, delta_low, flags)):
            extra = jnp.where(row == n, part.astype(F32), extra)
        out_ref[a, 2 * TOK :, :ROWS] = extra.astype(BF16)
        out_ref[a, 2 * TOK :, ROWS:] = jnp.zeros((EXTRA, wide - ROWS), BF16)
    for copy in copies[1]:
        copy.wait()


def attention_kernel(keep_ref, span_ref, message_ref, start_ref, *refs):
    kv_refs, refs = refs[:ZS], refs[ZS:]
    dq_ref, refs = refs[0], refs[1:]
    dkv_refs, refs = refs[:ZS], refs[ZS:]
    acc_ref, kt_ref, q_ref, g_ref, qt_ref, gt_ref, dqt_ref = refs
    z = lax.axis_index("z")
    sources = [lax.rem(z - off + ZS, ZS) for off in OFFSETS]
    lane_token = lax.rem(lax.broadcasted_iota(jnp.int32, (1, ROWS), 1), TOK)
    sublane = lax.broadcasted_iota(jnp.int32, (TOK, ROWS), 0)

    def keys_of(b, lanes):
        return jnp.concatenate(
            [kv[b * PAIR + c, :, lanes] for c in range(PAIR) for kv in kv_refs], axis=0
        )

    def prepare(b, _):
        kt_ref[b] = keys_of(b, pl.ds(0, HD)).T
        acc_ref[b] = jnp.zeros((PAIR * CHUNK, 2 * HD), F32)
        return 0

    lax.fori_loop(0, AS // PAIR, prepare, 0)

    def pair_of_chunks(j, _):
        lse, delta, start, q_pos = [], [], [], []
        for c in range(PAIR):
            i = j * PAIR + c
            for h in range(GROUP):
                rows = pl.ds(c * ROWS + h * TOK, TOK)
                q_ref[rows, :] = message_ref[i, :TOK, h * HD : (h + 1) * HD]
                g_ref[rows, :] = message_ref[i, TOK : 2 * TOK, h * HD : (h + 1) * HD]
            extra = message_ref[i, 2 * TOK :, :ROWS].astype(F32)
            lse.append(extra[0:1] + extra[1:2])
            delta.append(extra[2:3] + extra[3:4])
            start.append(start_ref[i])
            q_pos.append(i * CHUNK + z * TOK + lane_token)
        qt_ref[...] = q_ref[...].T
        gt_ref[...] = g_ref[...].T
        dqt_ref[...] = jnp.zeros((HD, PAIR * ROWS), F32)

        def tile(b, masked):
            scores = jnp.dot(keys_of(b, pl.ds(0, HD)), qt_ref[...], preferred_element_type=F32)
            dprobs = jnp.dot(keys_of(b, pl.ds(HD, HD)), gt_ref[...], preferred_element_type=F32)
            probs_b, dscores_b = [], []
            for k in range(PAIR * ZS):
                a, r = b * PAIR + k // ZS, k % ZS
                rows = slice(k * TOK, (k + 1) * TOK)
                probs_row, dscores_row = [], []
                for c in range(PAIR):
                    i = j * PAIR + c
                    columns = slice(c * ROWS, (c + 1) * ROWS)
                    distance = 2 * (i - a) + z // 4 - sources[r] // 4
                    kept = keep_ref[i, jnp.maximum(distance, 0)] > 0
                    shift = lse[c] + jnp.where(kept, 0.0, BIG)
                    probs = jnp.exp2(scores[rows, columns] * (SCALE * LOG2E) - shift)
                    if masked:
                        k_pos = a * CHUNK + sources[r] * TOK + sublane
                        probs = jnp.where((k_pos >= start[c]) & (k_pos <= q_pos[c]), probs, 0.0)
                    probs_row.append(probs.astype(BF16))
                    dscores_row.append((probs * (dprobs[rows, columns] - delta[c])).astype(BF16))
                probs_b.append(jnp.concatenate(probs_row, axis=1))
                dscores_b.append(jnp.concatenate(dscores_row, axis=1))
            probs_b = jnp.concatenate(probs_b, axis=0)
            dscores_b = jnp.concatenate(dscores_b, axis=0)
            acc_ref[b, :, :HD] += jnp.dot(dscores_b, q_ref[...], preferred_element_type=F32)
            acc_ref[b, :, HD:] += jnp.dot(probs_b, g_ref[...], preferred_element_type=F32)
            dqt_ref[...] += jnp.dot(kt_ref[b], dscores_b, preferred_element_type=F32)

        def step(b, _):
            masked = (b == j) | (span_ref[j * PAIR + PAIR - 1, 1] > b * PAIR * CHUNK)

            @pl.when(masked)
            def _():
                tile(b, True)

            @pl.when(jnp.logical_not(masked))
            def _():
                tile(b, False)

            return 0

        lax.fori_loop(span_ref[j * PAIR, 0] // (PAIR * CHUNK), j + 1, step, 0)
        dq = (dqt_ref[...] * SCALE).T.astype(BF16)
        for c in range(PAIR):
            for h in range(GROUP):
                first = c * ROWS + h * TOK
                dq_ref[j * PAIR + c, :, h * HD : (h + 1) * HD] = dq[first : first + TOK]
        return 0

    lax.fori_loop(0, AS // PAIR, pair_of_chunks, 0)

    def finish(b, _):
        for k in range(PAIR * ZS):
            piece = acc_ref[b, k * TOK : (k + 1) * TOK, :]
            out = dkv_refs[k % ZS].at[b * PAIR + k // ZS]
            out[:, :HD] = (piece[:, :HD] * SCALE).astype(BF16)
            out[:, HD:] = piece[:, HD:].astype(BF16)
        return 0

    lax.fori_loop(0, AS // PAIR, finish, 0)


def sum_kernel(*refs):
    total = refs[0][...].astype(F32)
    for ref in refs[1:-1]:
        total = total + ref[...].astype(F32)
    refs[-1][...] = total.astype(BF16)


def unpack_queries_kernel(in_ref, out_ref, sems):
    wide = GROUP * HD
    run_copies(
        [
            pltpu.make_async_copy(in_ref.at[a], out_ref.at[:, pl.ds(a * wide, wide)], sems.at[a])
            for a in range(AS)
        ]
    )


def unpack_kv_kernel(in_ref, dk_ref, dv_ref, sems):
    run_copies(
        [
            pltpu.make_async_copy(
                in_ref.at[a, :, pl.ds(n * HD, HD)], ref.at[:, pl.ds(a * HD, HD)], sems.at[n, a]
            )
            for n, ref in enumerate((dk_ref, dv_ref))
            for a in range(AS)
        ]
    )


def in_hbm():
    return pl.BlockSpec(memory_space=pltpu.HBM)


def anywhere():
    return pl.BlockSpec(memory_space=pl.ANY)


def in_vmem():
    return pl.BlockSpec(memory_space=pltpu.VMEM)


def in_smem():
    return pl.BlockSpec(memory_space=pltpu.SMEM)


def partial_sum(*values):
    shape = values[0].shape
    return pl.pallas_call(
        sum_kernel,
        out_shape=jax.ShapeDtypeStruct(shape, BF16),
        in_specs=[in_vmem()] * len(values),
        out_specs=in_vmem(),
        compiler_params=pltpu.CompilerParams(vmem_limit_bytes=4 * 2**20),
        cost_estimate=pl.CostEstimate(
            flops=65536 * len(values), bytes_accessed=131072 * (1 + len(values)), transcendentals=0
        ),
    )(*values)


def shards(query, key, value, output, out_grad, lse, doc_lengths, block_keep):
    i32 = jnp.int32
    z = lax.axis_index("z").astype(i32)
    columns = GROUP * HD
    dma = pltpu.SemaphoreType.DMA
    small_kernel = pltpu.CompilerParams(vmem_limit_bytes=4 * 2**20)

    kv_send = pl.pallas_call(
        pack_kv_kernel,
        out_shape=jax.ShapeDtypeStruct((AS, TOK, 2 * HD), BF16),
        in_specs=[in_hbm(), in_hbm()],
        out_specs=anywhere(),
        scratch_shapes=[dma((2, AS))],
        compiler_params=small_kernel,
        cost_estimate=pl.CostEstimate(flops=0, bytes_accessed=262144, transcendentals=0),
    )(key, value)
    kv_own = exchange(kv_send)

    reach = block_keep.shape[1]
    message_send = pl.pallas_call(
        pack_queries_kernel,
        out_shape=jax.ShapeDtypeStruct((AS, 2 * TOK + EXTRA, columns), BF16),
        in_specs=[in_hbm()] * 5,
        out_specs=in_vmem(),
        scratch_shapes=[
            pltpu.VMEM((TOK, AS * columns), BF16),
            pltpu.VMEM(lse.shape, F32),
            pltpu.VMEM(block_keep.shape, i32),
            pltpu.VMEM((8, ROWS), F32),
            dma((3, AS)),
            dma((2,)),
        ],
        compiler_params=pltpu.CompilerParams(vmem_limit_bytes=8 * 2**20),
        cost_estimate=pl.CostEstimate(flops=67108864, bytes_accessed=2800000, transcendentals=0),
    )(query, out_grad, output, lse, block_keep)
    message = exchange(message_send)

    pieces = {0: kv_own}
    for off in (1, -1, 2, -2):
        pieces[off] = along_z(kv_own, off)
    pieces[3] = along_z(pieces[2], 1)
    pieces[-3] = along_z(pieces[-2], -1)
    pieces[4] = along_z(pieces[2], 2)

    keep = message[:, 2 * TOK + 4, :reach].astype(i32)
    ends = jnp.arange(doc_lengths.shape[0], dtype=i32)
    starts = jnp.sum(jnp.where(ends[None, :] < ends[:, None], doc_lengths[None, :], 0), axis=1)
    base = lax.axis_index("y").astype(i32) * WINDOW
    positions = (
        base
        + jnp.arange(AS, dtype=i32)[:, None] * CHUNK
        + z * TOK
        + (jnp.arange(ROWS, dtype=i32) % TOK)[None, :]
    )
    start_of = jnp.max(
        jnp.where(starts[None, None, :] <= positions[:, :, None], starts[None, None, :], 0), axis=2
    )
    start_of = jnp.maximum(start_of - base, 0)
    span = jnp.stack([start_of[:, 0], start_of[:, TOK - 1]], axis=1)

    piece_shape = jax.ShapeDtypeStruct((AS, TOK, 2 * HD), BF16)
    results = pl.pallas_call(
        attention_kernel,
        out_shape=[jax.ShapeDtypeStruct((AS, TOK, columns), BF16)] + [piece_shape] * ZS,
        in_specs=[in_smem()] * 2 + [in_vmem()] * (2 + ZS),
        out_specs=[in_vmem()] * (1 + ZS),
        scratch_shapes=[
            pltpu.VMEM((AS // PAIR, PAIR * CHUNK, 2 * HD), F32),
            pltpu.VMEM((AS // PAIR, HD, PAIR * CHUNK), BF16),
            pltpu.VMEM((PAIR * ROWS, HD), BF16),
            pltpu.VMEM((PAIR * ROWS, HD), BF16),
            pltpu.VMEM((HD, PAIR * ROWS), BF16),
            pltpu.VMEM((HD, PAIR * ROWS), BF16),
            pltpu.VMEM((HD, PAIR * ROWS), F32),
        ],
        compiler_params=pltpu.CompilerParams(vmem_limit_bytes=24 * 2**20),
        cost_estimate=pl.CostEstimate(
            flops=3000000000, bytes_accessed=4000000, transcendentals=2360000
        ),
    )(keep, span, message, start_of.reshape(AS, 1, ROWS), *[pieces[o] for o in OFFSETS])
    dq, part = results[0], dict(zip(OFFSETS, results[1:]))

    from_three, from_four = along_z(part[3], -1), along_z(part[4], -2)
    from_minus_three = along_z(part[-3], 1)
    dq_back = exchange(dq)
    one, minus_one = along_z(part[1], -1), along_z(part[-1], 1)
    two = along_z(partial_sum(part[2], from_three, from_four), -2)
    minus_two = along_z(partial_sum(part[-2], from_minus_three), 2)
    returned = (part[0], one, minus_one, two, minus_two)
    returned, dq_back = lax.optimization_barrier((returned, dq_back))
    query_grad = pl.pallas_call(
        unpack_queries_kernel,
        out_shape=jax.ShapeDtypeStruct((TOK, AS * columns), BF16),
        in_specs=[anywhere()],
        out_specs=anywhere(),
        scratch_shapes=[dma((AS,))],
        compiler_params=small_kernel,
        cost_estimate=pl.CostEstimate(flops=0, bytes_accessed=1048576, transcendentals=0),
    )(dq_back)
    grads = exchange(partial_sum(*returned))
    half = jax.ShapeDtypeStruct((TOK, KVH * HD), BF16)
    key_grad, value_grad = pl.pallas_call(
        unpack_kv_kernel,
        out_shape=[half, half],
        in_specs=[anywhere()],
        out_specs=[anywhere(), anywhere()],
        scratch_shapes=[dma((2, AS))],
        compiler_params=small_kernel,
        cost_estimate=pl.CostEstimate(flops=0, bytes_accessed=262144, transcendentals=0),
    )(grads)
    return (query_grad, key_grad, value_grad)


def solution(mesh):
    fine = Mesh(mesh.devices.reshape(4, 2, 2, 2, ZS), ("y", "xl", "c", "xh", "z"))
    tokens = P(("y", "xl", "c", "xh", "z"), None)
    in_specs = (tokens,) * 6 + (P(), P(("y", "xl", "c"), None))
    return jax.shard_map(
        shards, mesh=fine, in_specs=in_specs, out_specs=(tokens,) * 3, check_vma=False
    )
```

```python
import functools
import math

import jax
import jax.numpy as jnp
from jax import lax
from jax.experimental import pallas as pl
from jax.experimental.pallas import tpu as pltpu
from jax.sharding import Mesh
from jax.sharding import PartitionSpec as P

KVH = 8
HD = 128
GROUP = 8
BLOCK = 128
WINDOW = 2048
TOK = 32
ZS = 8
AS = 8
CHUNK = TOK * ZS
ROWS = TOK * GROUP
SCALE = 1.0 / math.sqrt(HD)
LOG2E = math.log2(math.e)
BIG = 1e30
PAIR = 2
SPAN = 4
EXTRA = 8
HEADS = ("xl", "c", "xh")
F32 = jnp.float32
BF16 = jnp.bfloat16
FAR = (3, -3, 4, 2)
NEAR = (0, 1, -1, -2)


def along_z(value, by):
    return lax.ppermute(value, "z", [(i, (i + by) % ZS) for i in range(ZS)])


def exchange(value):
    return lax.all_to_all(value, HEADS, split_axis=0, concat_axis=0, tiled=True)


def run_copies(copies):
    for copy in copies:
        copy.start()
    for copy in copies:
        copy.wait()


def pack_kv_kernel(k_ref, v_ref, out_ref, sems):
    run_copies(
        [
            pltpu.make_async_copy(
                ref.at[:, pl.ds(a * HD, HD)], out_ref.at[a, :, pl.ds(n * HD, HD)], sems.at[n, a]
            )
            for n, ref in enumerate((k_ref, v_ref))
            for a in range(AS)
        ]
    )


def split(value):
    high = value.astype(BF16)
    return high, (value - high.astype(F32)).astype(BF16)


def pack_queries_kernel(
    q_hbm, g_hbm, o_hbm, lse_hbm, keep_hbm, out_ref, o_ref, lse_ref, keep_ref, row_ref, sems, small
):
    wide = GROUP * HD
    copies = [[], []]
    small_copies = [
        pltpu.make_async_copy(lse_hbm, lse_ref, small.at[0]),
        pltpu.make_async_copy(keep_hbm, keep_ref, small.at[1]),
    ]
    for copy in small_copies:
        copy.start()
    for a in range(AS):
        columns = pl.ds(a * wide, wide)
        for n, (src, dst) in enumerate(
            (
                (g_hbm, out_ref.at[a, pl.ds(TOK, TOK), :]),
                (o_hbm, o_ref.at[:, columns]),
            )
        ):
            copies[0].append(pltpu.make_async_copy(src.at[:, columns], dst, sems.at[n, a]))
        copies[1].append(
            pltpu.make_async_copy(
                q_hbm.at[:, columns], out_ref.at[a, pl.ds(0, TOK), :], sems.at[2, a]
            )
        )
    for copy in copies[0] + copies[1]:
        copy.start()
    ones = jnp.ones((EXTRA, 2 * HD), BF16)
    lane = lax.broadcasted_iota(jnp.int32, (TOK, ROWS), 1)
    spread = (lane % TOK == lax.broadcasted_iota(jnp.int32, (TOK, ROWS), 0)).astype(F32).astype(BF16)
    head_lane = lax.broadcasted_iota(jnp.int32, (GROUP, ROWS), 1) // TOK
    own_head = head_lane == lax.broadcasted_iota(jnp.int32, (GROUP, ROWS), 0)
    row = lax.broadcasted_iota(jnp.int32, (EXTRA, ROWS), 0)
    for copy in small_copies:
        copy.wait()
    place = lax.axis_index("xh") * 2 + lax.axis_index("z") // 4
    kept = keep_ref[...].astype(F32)
    at_place = lax.broadcasted_iota(jnp.int32, kept.shape, 0) == place
    row_ref[...] = jnp.zeros(row_ref.shape, F32)
    row_ref[0:1, : kept.shape[1]] = jnp.sum(jnp.where(at_place, kept, 0.0), axis=0, keepdims=True)
    flags = row_ref[0:1]
    scaled = lse_ref[...].T * LOG2E
    high, low = split(scaled)
    lower = split(scaled - high.astype(F32) - low.astype(F32))[0]
    lse_all = sum(jnp.dot(p, spread, preferred_element_type=F32) for p in (high, low, lower))
    for a in range(AS):
        copies[0][2 * a].wait()
        copies[0][2 * a + 1].wait()
        columns = slice(a * wide, (a + 1) * wide)
        product = out_ref[a, TOK : 2 * TOK, :].astype(F32) * o_ref[:, columns].astype(F32)
        high, low = split(product)
        stacked = jnp.concatenate(
            [
                jnp.concatenate([p[:, h * HD : (h + 1) * HD] for h in range(GROUP)], axis=0)
                for p in (high, low)
            ],
            axis=1,
        )
        delta = lax.dot_general(
            ones, stacked, (((1,), (1,)), ((), ())), preferred_element_type=F32
        )[:1]
        lse = jnp.sum(
            jnp.where(own_head, lse_all[a * GROUP : (a + 1) * GROUP], 0.0), axis=0, keepdims=True
        )
        lse_high, lse_low = split(lse)
        delta_high, delta_low = split(delta)
        extra = jnp.zeros((EXTRA, ROWS), F32)
        for n, part in enumerate((lse_high, lse_low, delta_high, delta_low, flags)):
            extra = jnp.where(row == n, part.astype(F32), extra)
        out_ref[a, 2 * TOK :, :ROWS] = extra.astype(BF16)
        out_ref[a, 2 * TOK :, ROWS:] = jnp.zeros((EXTRA, wide - ROWS), BF16)
    for copy in copies[1]:
        copy.wait()


def attention_kernel(offsets, final, keep_ref, span_ref, message_ref, start_ref, *refs):
    pieces = len(offsets)
    kv_refs, refs = refs[:pieces], refs[pieces:]
    if final:
        dqt_in_ref, refs = refs[0], refs[1:]
    dq_ref, refs = refs[0], refs[1:]
    dkv_refs, refs = refs[:pieces], refs[pieces:]
    acc_ref, kt_ref, q_ref, g_ref, qt_ref, gt_ref, dqt_ref = refs
    z = lax.axis_index("z")
    sources = [lax.rem(z - off + ZS, ZS) for off in offsets]
    lane_token = lax.rem(lax.broadcasted_iota(jnp.int32, (1, ROWS), 1), TOK)
    sublane = lax.broadcasted_iota(jnp.int32, (TOK, ROWS), 0)
    keys = SPAN * pieces * TOK

    def keys_of(b, lanes):
        return jnp.concatenate(
            [kv[b * SPAN + c, :, lanes] for c in range(SPAN) for kv in kv_refs], axis=0
        )

    def prepare(b, _):
        kt_ref[b] = keys_of(b, pl.ds(0, HD)).T
        acc_ref[b] = jnp.zeros((keys, 2 * HD), F32)
        return 0

    lax.fori_loop(0, AS // SPAN, prepare, 0)

    def pair_of_chunks(j, _):
        lse, delta, start, q_pos = [], [], [], []
        for c in range(PAIR):
            i = j * PAIR + c
            for h in range(GROUP):
                rows = pl.ds(c * ROWS + h * TOK, TOK)
                q_ref[rows, :] = message_ref[i, :TOK, h * HD : (h + 1) * HD]
                g_ref[rows, :] = message_ref[i, TOK : 2 * TOK, h * HD : (h + 1) * HD]
            extra = message_ref[i, 2 * TOK :, :ROWS].astype(F32)
            lse.append(extra[0:1] + extra[1:2])
            delta.append(extra[2:3] + extra[3:4])
            start.append(start_ref[i])
            q_pos.append(i * CHUNK + z * TOK + lane_token)
        qt_ref[...] = q_ref[...].T
        gt_ref[...] = g_ref[...].T
        if final:
            dqt_ref[...] = dqt_in_ref[j]
        else:
            dqt_ref[...] = jnp.zeros((HD, PAIR * ROWS), F32)

        def tile(b, masked):
            scores = jnp.dot(keys_of(b, pl.ds(0, HD)), qt_ref[...], preferred_element_type=F32)
            dprobs = jnp.dot(keys_of(b, pl.ds(HD, HD)), gt_ref[...], preferred_element_type=F32)
            probs_b, dscores_b = [], []
            for k in range(SPAN * pieces):
                a, r = b * SPAN + k // pieces, k % pieces
                rows = slice(k * TOK, (k + 1) * TOK)
                probs_row, dscores_row = [], []
                for c in range(PAIR):
                    i = j * PAIR + c
                    columns = slice(c * ROWS, (c + 1) * ROWS)
                    distance = 2 * (i - a) + z // 4 - sources[r] // 4
                    kept = keep_ref[i, jnp.maximum(distance, 0)] > 0
                    shift = lse[c] + jnp.where(kept, 0.0, BIG)
                    probs = jnp.exp2(scores[rows, columns] * (SCALE * LOG2E) - shift)
                    if masked:
                        k_pos = a * CHUNK + sources[r] * TOK + sublane
                        probs = jnp.where((k_pos >= start[c]) & (k_pos <= q_pos[c]), probs, 0.0)
                    probs_row.append(probs.astype(BF16))
                    dscores_row.append((probs * (dprobs[rows, columns] - delta[c])).astype(BF16))
                probs_b.append(jnp.concatenate(probs_row, axis=1))
                dscores_b.append(jnp.concatenate(dscores_row, axis=1))
            probs_b = jnp.concatenate(probs_b, axis=0)
            dscores_b = jnp.concatenate(dscores_b, axis=0)
            acc_ref[b, :, :HD] += jnp.dot(dscores_b, q_ref[...], preferred_element_type=F32)
            acc_ref[b, :, HD:] += jnp.dot(probs_b, g_ref[...], preferred_element_type=F32)
            dqt_ref[...] += jnp.dot(kt_ref[b], dscores_b, preferred_element_type=F32)

        def step(b, _):
            reaches_own = (b + 1) * SPAN > j * PAIR
            masked = reaches_own | (span_ref[j * PAIR + PAIR - 1, 1] > b * SPAN * CHUNK)

            @pl.when(masked)
            def _():
                tile(b, True)

            @pl.when(jnp.logical_not(masked))
            def _():
                tile(b, False)

            return 0

        first = span_ref[j * PAIR, 0] // (SPAN * CHUNK)
        lax.fori_loop(first, (j * PAIR + PAIR - 1) // SPAN + 1, step, 0)
        if not final:
            dq_ref[j] = dqt_ref[...]
            return 0
        dq = (dqt_ref[...] * SCALE).T.astype(BF16)
        for c in range(PAIR):
            for h in range(GROUP):
                at = c * ROWS + h * TOK
                dq_ref[j * PAIR + c, :, h * HD : (h + 1) * HD] = dq[at : at + TOK]
        return 0

    lax.fori_loop(0, AS // PAIR, pair_of_chunks, 0)

    def finish(b, _):
        for k in range(SPAN * pieces):
            piece = acc_ref[b, k * TOK : (k + 1) * TOK, :]
            out = dkv_refs[k % pieces].at[b * SPAN + k // pieces]
            out[:, :HD] = (piece[:, :HD] * SCALE).astype(BF16)
            out[:, HD:] = piece[:, HD:].astype(BF16)
        return 0

    lax.fori_loop(0, AS // SPAN, finish, 0)


def attention(offsets, scalars, message, start, kv, dqt=None):
    final = dqt is not None
    pieces = len(offsets)
    keys = SPAN * pieces * TOK
    rows = PAIR * ROWS
    dqt_shape = jax.ShapeDtypeStruct((AS // PAIR, HD, rows), F32)
    dq_shape = jax.ShapeDtypeStruct((AS, TOK, GROUP * HD), BF16)
    results = pl.pallas_call(
        functools.partial(attention_kernel, offsets, final),
        out_shape=[dq_shape if final else dqt_shape]
        + [jax.ShapeDtypeStruct((AS, TOK, 2 * HD), BF16)] * pieces,
        in_specs=[in_smem()] * 2 + [in_vmem()] * (2 + pieces + final),
        out_specs=[in_vmem()] * (1 + pieces),
        scratch_shapes=[
            pltpu.VMEM((AS // SPAN, keys, 2 * HD), F32),
            pltpu.VMEM((AS // SPAN, HD, keys), BF16),
            pltpu.VMEM((rows, HD), BF16),
            pltpu.VMEM((rows, HD), BF16),
            pltpu.VMEM((HD, rows), BF16),
            pltpu.VMEM((HD, rows), BF16),
            pltpu.VMEM((HD, rows), F32),
        ],
        compiler_params=pltpu.CompilerParams(vmem_limit_bytes=24 * 2**20),
        cost_estimate=pl.CostEstimate(
            flops=400000000 * pieces, bytes_accessed=3000000, transcendentals=300000 * pieces
        ),
    )(*scalars, message, start, *[kv[o] for o in offsets], *([dqt] if final else []))
    return results[0], dict(zip(offsets, results[1:]))


def sum_kernel(*refs):
    total = refs[0][...].astype(F32)
    for ref in refs[1:-1]:
        total = total + ref[...].astype(F32)
    refs[-1][...] = total.astype(BF16)


def pack_gradients_kernel(dq_ref, *refs):
    pieces, (out_ref, rows_ref, sems) = refs[:-3], refs[-3:]
    dq_copy = pltpu.make_async_copy(dq_ref, out_ref.at[:, pl.ds(0, TOK), :], sems.at[0])
    dq_copy.start()
    total = pieces[0][...].astype(F32)
    for piece in pieces[1:]:
        total = total + piece[...].astype(F32)
    total = total.astype(BF16)
    for n in range(TOK // 8):
        rows_ref[:, :, n * 2 * HD : (n + 1) * 2 * HD] = total[:, n * 8 : (n + 1) * 8, :]
    rows_copy = pltpu.make_async_copy(rows_ref, out_ref.at[:, pl.ds(TOK, 8), :], sems.at[1])
    rows_copy.start()
    dq_copy.wait()
    rows_copy.wait()


def unpack_gradients_kernel(in_ref, dq_ref, dk_ref, dv_ref, sems, small):
    wide = GROUP * HD
    run_copies(
        [
            pltpu.make_async_copy(
                in_ref.at[a, pl.ds(0, TOK), :], dq_ref.at[:, pl.ds(a * wide, wide)], sems.at[a]
            )
            for a in range(AS)
        ]
        + [
            pltpu.make_async_copy(
                in_ref.at[a, pl.ds(TOK, 8), pl.ds((2 * n + m) * HD, HD)],
                ref.at[pl.ds(n * 8, 8), pl.ds(a * HD, HD)],
                small.at[m, n, a],
            )
            for a in range(AS)
            for n in range(TOK // 8)
            for m, ref in enumerate((dk_ref, dv_ref))
        ]
    )


def in_hbm():
    return pl.BlockSpec(memory_space=pltpu.HBM)


def held_in_hbm(*values):
    return [pltpu.with_memory_space_constraint(v, pltpu.HBM) for v in values]


def anywhere():
    return pl.BlockSpec(memory_space=pl.ANY)


def in_vmem():
    return pl.BlockSpec(memory_space=pltpu.VMEM)


def in_smem():
    return pl.BlockSpec(memory_space=pltpu.SMEM)


def partial_sum(*values):
    shape = values[0].shape
    return pl.pallas_call(
        sum_kernel,
        out_shape=jax.ShapeDtypeStruct(shape, BF16),
        in_specs=[in_vmem()] * len(values),
        out_specs=in_vmem(),
        compiler_params=pltpu.CompilerParams(vmem_limit_bytes=4 * 2**20),
        cost_estimate=pl.CostEstimate(
            flops=65536 * len(values), bytes_accessed=131072 * (1 + len(values)), transcendentals=0
        ),
    )(*values)


def shards(query, key, value, output, out_grad, lse, doc_lengths, block_keep):
    i32 = jnp.int32
    z = lax.axis_index("z").astype(i32)
    columns = GROUP * HD
    dma = pltpu.SemaphoreType.DMA
    small_kernel = pltpu.CompilerParams(vmem_limit_bytes=4 * 2**20)

    kv_send = pl.pallas_call(
        pack_kv_kernel,
        out_shape=jax.ShapeDtypeStruct((AS, TOK, 2 * HD), BF16),
        in_specs=[in_hbm(), in_hbm()],
        out_specs=anywhere(),
        scratch_shapes=[dma((2, AS))],
        compiler_params=small_kernel,
        cost_estimate=pl.CostEstimate(flops=0, bytes_accessed=262144, transcendentals=0),
    )(*held_in_hbm(key, value))
    kv_own = exchange(kv_send)

    reach = block_keep.shape[1]
    message_send = pl.pallas_call(
        pack_queries_kernel,
        out_shape=jax.ShapeDtypeStruct((AS, 2 * TOK + EXTRA, columns), BF16),
        in_specs=[in_hbm()] * 5,
        out_specs=in_vmem(),
        scratch_shapes=[
            pltpu.VMEM((TOK, AS * columns), BF16),
            pltpu.VMEM(lse.shape, F32),
            pltpu.VMEM(block_keep.shape, i32),
            pltpu.VMEM((8, ROWS), F32),
            dma((3, AS)),
            dma((2,)),
        ],
        compiler_params=pltpu.CompilerParams(vmem_limit_bytes=8 * 2**20),
        cost_estimate=pl.CostEstimate(flops=67108864, bytes_accessed=2800000, transcendentals=0),
    )(*held_in_hbm(query, out_grad, output, lse, block_keep))
    message = exchange(message_send)

    pieces = {0: kv_own}
    for off in (1, -1, 2, -2):
        pieces[off] = along_z(kv_own, off)
    pieces[3] = along_z(pieces[2], 1)
    pieces[-3] = along_z(pieces[-2], -1)
    pieces[4] = along_z(pieces[2], 2)

    keep = message[:, 2 * TOK + 4, :reach].astype(i32)
    ends = jnp.arange(doc_lengths.shape[0], dtype=i32)
    starts = jnp.sum(jnp.where(ends[None, :] < ends[:, None], doc_lengths[None, :], 0), axis=1)
    base = lax.axis_index("y").astype(i32) * WINDOW
    positions = (
        base
        + jnp.arange(AS, dtype=i32)[:, None] * CHUNK
        + z * TOK
        + (jnp.arange(ROWS, dtype=i32) % TOK)[None, :]
    )
    start_of = jnp.max(
        jnp.where(starts[None, None, :] <= positions[:, :, None], starts[None, None, :], 0), axis=2
    )
    start_of = jnp.maximum(start_of - base, 0)
    span = jnp.stack([start_of[:, 0], start_of[:, TOK - 1]], axis=1)

    scalars, start = (keep, span), start_of.reshape(AS, 1, ROWS)
    dqt, part = attention(FAR, scalars, message, start, pieces)
    from_three, from_four = along_z(part[3], -1), along_z(part[4], -2)
    from_minus_three = along_z(part[-3], 1)
    dq, near_part = attention(NEAR, scalars, message, start, pieces, dqt)
    part.update(near_part)
    one, minus_one = along_z(part[1], -1), along_z(part[-1], 1)
    two = along_z(partial_sum(part[2], from_three, from_four), -2)
    minus_two = along_z(partial_sum(part[-2], from_minus_three), 2)
    gradients_send = pl.pallas_call(
        pack_gradients_kernel,
        out_shape=jax.ShapeDtypeStruct((AS, TOK + 8, columns), BF16),
        in_specs=[anywhere()] + [in_vmem()] * 5,
        out_specs=anywhere(),
        scratch_shapes=[pltpu.VMEM((AS, 8, columns), BF16), dma((2,))],
        compiler_params=small_kernel,
        cost_estimate=pl.CostEstimate(flops=400000, bytes_accessed=1900000, transcendentals=0),
    )(dq, part[0], one, minus_one, two, minus_two)
    half = jax.ShapeDtypeStruct((TOK, KVH * HD), BF16)
    return pl.pallas_call(
        unpack_gradients_kernel,
        out_shape=[jax.ShapeDtypeStruct((TOK, AS * columns), BF16), half, half],
        in_specs=[anywhere()],
        out_specs=[anywhere()] * 3,
        scratch_shapes=[dma((AS,)), dma((2, TOK // 8, AS))],
        compiler_params=small_kernel,
        cost_estimate=pl.CostEstimate(flops=0, bytes_accessed=1300000, transcendentals=0),
    )(exchange(gradients_send))


def solution(mesh):
    fine = Mesh(mesh.devices.reshape(4, 2, 2, 2, ZS), ("y", "xl", "c", "xh", "z"))
    tokens = P(("y", "xl", "c", "xh", "z"), None)
    in_specs = (tokens,) * 6 + (P(), P(("y", "xl", "c"), None))
    return jax.shard_map(
        shards, mesh=fine, in_specs=in_specs, out_specs=(tokens,) * 3, check_vma=False
    )
```

```python
import functools
import math

import jax
import jax.numpy as jnp
from jax import lax
from jax.experimental import pallas as pl
from jax.experimental.pallas import tpu as pltpu
from jax.sharding import Mesh
from jax.sharding import PartitionSpec as P

KVH = 8
HD = 128
GROUP = 8
BLOCK = 128
WINDOW = 2048
TOK = 32
ZS = 8
AS = 8
CHUNK = TOK * ZS
ROWS = TOK * GROUP
SCALE = 1.0 / math.sqrt(HD)
LOG2E = math.log2(math.e)
BIG = 1e30
PAIR = 2
SPAN = 4
EXTRA = 8
HEADS = ("xl", "c", "xh")
F32 = jnp.float32
BF16 = jnp.bfloat16
FAR = (3, -3, 4, 2)
NEAR = (0, 1, -1, -2)


def along_z(value, by):
    return lax.ppermute(value, "z", [(i, (i + by) % ZS) for i in range(ZS)])


def exchange(value):
    return lax.all_to_all(value, HEADS, split_axis=0, concat_axis=0, tiled=True)


def own_place():
    return (lax.axis_index("xl") * 2 + lax.axis_index("c")) * 2 + lax.axis_index("xh")


def shifted(value, by):
    return lax.ppermute(value, HEADS, [(i, (i + by) % AS) for i in range(AS)])


def pack_kv_kernel(k_hbm, v_hbm, out_ref, k_ref, v_ref, sems):
    copies = [
        pltpu.make_async_copy(k_hbm, k_ref, sems.at[0]),
        pltpu.make_async_copy(v_hbm, v_ref, sems.at[1]),
    ]
    for copy in copies:
        copy.start()
    for n, (copy, ref) in enumerate(zip(copies, (k_ref, v_ref))):
        copy.wait()
        for a in range(AS):
            out_ref[a, :, n * HD : (n + 1) * HD] = ref[:, a * HD : (a + 1) * HD]


def split(value):
    high = value.astype(BF16)
    return high, (value - high.astype(F32)).astype(BF16)


def pack_queries_kernel(
    q_hbm, g_hbm, o_hbm, lse_hbm, keep_hbm, out_ref, o_ref, lse_ref, keep_ref, row_ref, sems, small
):
    wide = GROUP * HD
    copies = [[], []]
    small_copies = [
        pltpu.make_async_copy(lse_hbm, lse_ref, small.at[0]),
        pltpu.make_async_copy(keep_hbm, keep_ref, small.at[1]),
    ]
    for copy in small_copies:
        copy.start()
    for a in range(AS):
        columns = pl.ds(a * wide, wide)
        for n, (src, dst) in enumerate(
            (
                (g_hbm, out_ref.at[a, pl.ds(TOK, TOK), :]),
                (o_hbm, o_ref.at[:, columns]),
            )
        ):
            copies[0].append(pltpu.make_async_copy(src.at[:, columns], dst, sems.at[n, a]))
        copies[1].append(
            pltpu.make_async_copy(
                q_hbm.at[:, columns], out_ref.at[a, pl.ds(0, TOK), :], sems.at[2, a]
            )
        )
    for copy in copies[0] + copies[1]:
        copy.start()
    ones = jnp.ones((EXTRA, 2 * HD), BF16)
    lane = lax.broadcasted_iota(jnp.int32, (TOK, ROWS), 1)
    spread = (lane % TOK == lax.broadcasted_iota(jnp.int32, (TOK, ROWS), 0)).astype(F32).astype(BF16)
    head_lane = lax.broadcasted_iota(jnp.int32, (GROUP, ROWS), 1) // TOK
    own_head = head_lane == lax.broadcasted_iota(jnp.int32, (GROUP, ROWS), 0)
    row = lax.broadcasted_iota(jnp.int32, (EXTRA, ROWS), 0)
    for copy in small_copies:
        copy.wait()
    place = lax.axis_index("xh") * 2 + lax.axis_index("z") // 4
    kept = keep_ref[...].astype(F32)
    at_place = lax.broadcasted_iota(jnp.int32, kept.shape, 0) == place
    row_ref[...] = jnp.zeros(row_ref.shape, F32)
    row_ref[0:1, : kept.shape[1]] = jnp.sum(jnp.where(at_place, kept, 0.0), axis=0, keepdims=True)
    flags = row_ref[0:1]
    scaled = lse_ref[...].T * LOG2E
    high, low = split(scaled)
    lower = split(scaled - high.astype(F32) - low.astype(F32))[0]
    lse_all = sum(jnp.dot(p, spread, preferred_element_type=F32) for p in (high, low, lower))
    for a in range(AS):
        copies[0][2 * a].wait()
        copies[0][2 * a + 1].wait()
        columns = slice(a * wide, (a + 1) * wide)
        product = out_ref[a, TOK : 2 * TOK, :].astype(F32) * o_ref[:, columns].astype(F32)
        high, low = split(product)
        stacked = jnp.concatenate(
            [
                jnp.concatenate([p[:, h * HD : (h + 1) * HD] for h in range(GROUP)], axis=0)
                for p in (high, low)
            ],
            axis=1,
        )
        delta = lax.dot_general(
            ones, stacked, (((1,), (1,)), ((), ())), preferred_element_type=F32
        )[:1]
        lse = jnp.sum(
            jnp.where(own_head, lse_all[a * GROUP : (a + 1) * GROUP], 0.0), axis=0, keepdims=True
        )
        lse_high, lse_low = split(lse)
        delta_high, delta_low = split(delta)
        extra = jnp.zeros((EXTRA, ROWS), F32)
        for n, part in enumerate((lse_high, lse_low, delta_high, delta_low, flags)):
            extra = jnp.where(row == n, part.astype(F32), extra)
        out_ref[a, 2 * TOK :, :ROWS] = extra.astype(BF16)
        out_ref[a, 2 * TOK :, ROWS:] = jnp.zeros((EXTRA, wide - ROWS), BF16)
    for copy in copies[1]:
        copy.wait()


def attention_kernel(offsets, final, keep_ref, span_ref, message_ref, start_ref, *refs):
    pieces = len(offsets)
    kv_refs, refs = refs[:pieces], refs[pieces:]
    if final:
        dqt_in_ref, refs = refs[0], refs[1:]
    dq_ref, refs = refs[0], refs[1:]
    dkv_refs, refs = refs[:pieces], refs[pieces:]
    acc_ref, kt_ref, q_ref, g_ref, qt_ref, gt_ref, dqt_ref = refs
    z = lax.axis_index("z")
    sources = [lax.rem(z - off + ZS, ZS) for off in offsets]
    lane_token = lax.rem(lax.broadcasted_iota(jnp.int32, (1, ROWS), 1), TOK)
    sublane = lax.broadcasted_iota(jnp.int32, (TOK, ROWS), 0)
    keys = SPAN * pieces * TOK

    def keys_of(b, lanes):
        return jnp.concatenate(
            [kv[b * SPAN + c, :, lanes] for c in range(SPAN) for kv in kv_refs], axis=0
        )

    def prepare(b, _):
        kt_ref[b] = keys_of(b, pl.ds(0, HD)).T
        acc_ref[b] = jnp.zeros((keys, 2 * HD), F32)
        return 0

    lax.fori_loop(0, AS // SPAN, prepare, 0)

    def pair_of_chunks(j, _):
        lse, delta, start, q_pos = [], [], [], []
        for c in range(PAIR):
            i = j * PAIR + c
            for h in range(GROUP):
                rows = pl.ds(c * ROWS + h * TOK, TOK)
                q_ref[rows, :] = message_ref[i, :TOK, h * HD : (h + 1) * HD]
                g_ref[rows, :] = message_ref[i, TOK : 2 * TOK, h * HD : (h + 1) * HD]
            extra = message_ref[i, 2 * TOK :, :ROWS].astype(F32)
            lse.append(extra[0:1] + extra[1:2])
            delta.append(extra[2:3] + extra[3:4])
            start.append(start_ref[i])
            q_pos.append(i * CHUNK + z * TOK + lane_token)
        qt_ref[...] = q_ref[...].T
        gt_ref[...] = g_ref[...].T
        if final:
            dqt_ref[...] = dqt_in_ref[j]
        else:
            dqt_ref[...] = jnp.zeros((HD, PAIR * ROWS), F32)

        def tile(b, masked):
            scores = jnp.dot(keys_of(b, pl.ds(0, HD)), qt_ref[...], preferred_element_type=F32)
            dprobs = jnp.dot(keys_of(b, pl.ds(HD, HD)), gt_ref[...], preferred_element_type=F32)
            probs_b, dscores_b = [], []
            for k in range(SPAN * pieces):
                a, r = b * SPAN + k // pieces, k % pieces
                rows = slice(k * TOK, (k + 1) * TOK)
                probs_row, dscores_row = [], []
                for c in range(PAIR):
                    i = j * PAIR + c
                    columns = slice(c * ROWS, (c + 1) * ROWS)
                    distance = 2 * (i - a) + z // 4 - sources[r] // 4
                    kept = keep_ref[i, jnp.maximum(distance, 0)] > 0
                    shift = lse[c] + jnp.where(kept, 0.0, BIG)
                    probs = jnp.exp2(scores[rows, columns] * (SCALE * LOG2E) - shift)
                    if masked:
                        k_pos = a * CHUNK + sources[r] * TOK + sublane
                        probs = jnp.where((k_pos >= start[c]) & (k_pos <= q_pos[c]), probs, 0.0)
                    probs_row.append(probs.astype(BF16))
                    dscores_row.append((probs * (dprobs[rows, columns] - delta[c])).astype(BF16))
                probs_b.append(jnp.concatenate(probs_row, axis=1))
                dscores_b.append(jnp.concatenate(dscores_row, axis=1))
            probs_b = jnp.concatenate(probs_b, axis=0)
            dscores_b = jnp.concatenate(dscores_b, axis=0)
            acc_ref[b, :, :HD] += jnp.dot(dscores_b, q_ref[...], preferred_element_type=F32)
            acc_ref[b, :, HD:] += jnp.dot(probs_b, g_ref[...], preferred_element_type=F32)
            dqt_ref[...] += jnp.dot(kt_ref[b], dscores_b, preferred_element_type=F32)

        def step(b, _):
            reaches_own = (b + 1) * SPAN > j * PAIR
            masked = reaches_own | (span_ref[j * PAIR + PAIR - 1, 1] > b * SPAN * CHUNK)

            @pl.when(masked)
            def _():
                tile(b, True)

            @pl.when(jnp.logical_not(masked))
            def _():
                tile(b, False)

            return 0

        first = span_ref[j * PAIR, 0] // (SPAN * CHUNK)
        lax.fori_loop(first, (j * PAIR + PAIR - 1) // SPAN + 1, step, 0)
        if not final:
            dq_ref[j] = dqt_ref[...]
            return 0
        dq = (dqt_ref[...] * SCALE).T.astype(BF16)
        for c in range(PAIR):
            for h in range(GROUP):
                at = c * ROWS + h * TOK
                dq_ref[j * PAIR + c, :, h * HD : (h + 1) * HD] = dq[at : at + TOK]
        return 0

    lax.fori_loop(0, AS // PAIR, pair_of_chunks, 0)

    def finish(b, _):
        for k in range(SPAN * pieces):
            piece = acc_ref[b, k * TOK : (k + 1) * TOK, :]
            out = dkv_refs[k % pieces].at[b * SPAN + k // pieces]
            out[:, :HD] = (piece[:, :HD] * SCALE).astype(BF16)
            out[:, HD:] = piece[:, HD:].astype(BF16)
        return 0

    lax.fori_loop(0, AS // SPAN, finish, 0)


def attention(offsets, scalars, message, start, kv, dqt=None):
    final = dqt is not None
    pieces = len(offsets)
    keys = SPAN * pieces * TOK
    rows = PAIR * ROWS
    dqt_shape = jax.ShapeDtypeStruct((AS // PAIR, HD, rows), F32)
    dq_shape = jax.ShapeDtypeStruct((AS, TOK, GROUP * HD), BF16)
    results = pl.pallas_call(
        functools.partial(attention_kernel, offsets, final),
        out_shape=[dq_shape if final else dqt_shape]
        + [jax.ShapeDtypeStruct((AS, TOK, 2 * HD), BF16)] * pieces,
        in_specs=[in_smem()] * 2 + [in_vmem()] * (2 + pieces + final),
        out_specs=[in_vmem()] * (1 + pieces),
        scratch_shapes=[
            pltpu.VMEM((AS // SPAN, keys, 2 * HD), F32),
            pltpu.VMEM((AS // SPAN, HD, keys), BF16),
            pltpu.VMEM((rows, HD), BF16),
            pltpu.VMEM((rows, HD), BF16),
            pltpu.VMEM((HD, rows), BF16),
            pltpu.VMEM((HD, rows), BF16),
            pltpu.VMEM((HD, rows), F32),
        ],
        compiler_params=pltpu.CompilerParams(vmem_limit_bytes=24 * 2**20),
        cost_estimate=pl.CostEstimate(
            flops=400000000 * pieces, bytes_accessed=3000000, transcendentals=300000 * pieces
        ),
    )(*scalars, message, start, *[kv[o] for o in offsets], *([dqt] if final else []))
    return results[0], dict(zip(offsets, results[1:]))


def sum_kernel(*refs):
    total = refs[0][...].astype(F32)
    for ref in refs[1:-1]:
        total = total + ref[...].astype(F32)
    refs[-1][...] = total.astype(BF16)


def pack_gradients_kernel(dq_ref, *refs):
    pieces, out_refs, (total_ref, sems) = refs[:5], refs[5 : 5 + AS], refs[5 + AS :]
    me = own_place()
    copies = []
    for k, out_ref in enumerate(out_refs):
        there = lax.rem(me + k, AS)
        copies.append(
            pltpu.make_async_copy(dq_ref.at[there], out_ref.at[pl.ds(0, TOK), :], sems.at[k])
        )
    for copy in copies:
        copy.start()
    total = pieces[0][...].astype(F32)
    for piece in pieces[1:]:
        total = total + piece[...].astype(F32)
    total_ref[...] = total.astype(BF16)
    for k, out_ref in enumerate(out_refs):
        there = lax.rem(me + k, AS)
        for n in range(TOK // 8):
            columns = slice(n * 2 * HD, (n + 1) * 2 * HD)
            out_ref[TOK:, columns] = total_ref[there, n * 8 : (n + 1) * 8, :]
    for copy in copies:
        copy.wait()


def unpack_gradients_kernel(*refs):
    in_refs, (dq_hbm, dk_hbm, dv_hbm, dk_ref, dv_ref, sems) = refs[:AS], refs[AS:]
    wide = GROUP * HD
    me = own_place()
    copies = []
    for k, in_ref in enumerate(in_refs):
        a = lax.rem(me - k + AS, AS)
        columns = pl.ds(pl.multiple_of(a * wide, wide), wide)
        copies.append(
            pltpu.make_async_copy(in_ref.at[pl.ds(0, TOK), :], dq_hbm.at[:, columns], sems.at[k])
        )
        copies[-1].start()
    for k, in_ref in enumerate(in_refs):
        a = lax.rem(me - k + AS, AS)
        columns = pl.ds(pl.multiple_of(a * HD, HD), HD)
        for n in range(TOK // 8):
            rows = slice(n * 8, (n + 1) * 8)
            dk_ref[rows, columns] = in_ref[TOK:, 2 * n * HD : (2 * n + 1) * HD]
            dv_ref[rows, columns] = in_ref[TOK:, (2 * n + 1) * HD : (2 * n + 2) * HD]
    copies.append(pltpu.make_async_copy(dk_ref, dk_hbm, sems.at[AS]))
    copies.append(pltpu.make_async_copy(dv_ref, dv_hbm, sems.at[AS + 1]))
    copies[-2].start()
    copies[-1].start()
    for copy in copies:
        copy.wait()


def in_hbm():
    return pl.BlockSpec(memory_space=pltpu.HBM)


def held_in_hbm(*values):
    return [pltpu.with_memory_space_constraint(v, pltpu.HBM) for v in values]


def anywhere():
    return pl.BlockSpec(memory_space=pl.ANY)


def in_vmem():
    return pl.BlockSpec(memory_space=pltpu.VMEM)


def in_smem():
    return pl.BlockSpec(memory_space=pltpu.SMEM)


def partial_sum(*values):
    shape = values[0].shape
    return pl.pallas_call(
        sum_kernel,
        out_shape=jax.ShapeDtypeStruct(shape, BF16),
        in_specs=[in_vmem()] * len(values),
        out_specs=in_vmem(),
        compiler_params=pltpu.CompilerParams(vmem_limit_bytes=4 * 2**20),
        cost_estimate=pl.CostEstimate(
            flops=65536 * len(values), bytes_accessed=131072 * (1 + len(values)), transcendentals=0
        ),
    )(*values)


def shards(query, key, value, output, out_grad, lse, doc_lengths, block_keep):
    i32 = jnp.int32
    z = lax.axis_index("z").astype(i32)
    columns = GROUP * HD
    dma = pltpu.SemaphoreType.DMA
    small_kernel = pltpu.CompilerParams(vmem_limit_bytes=4 * 2**20)

    kv_send = pl.pallas_call(
        pack_kv_kernel,
        out_shape=jax.ShapeDtypeStruct((AS, TOK, 2 * HD), BF16),
        in_specs=[in_hbm(), in_hbm()],
        out_specs=in_vmem(),
        scratch_shapes=[pltpu.VMEM(key.shape, BF16), pltpu.VMEM(key.shape, BF16), dma((2,))],
        compiler_params=small_kernel,
        cost_estimate=pl.CostEstimate(flops=0, bytes_accessed=262144, transcendentals=0),
    )(*held_in_hbm(key, value))
    kv_own = exchange(kv_send)

    reach = block_keep.shape[1]
    message_send = pl.pallas_call(
        pack_queries_kernel,
        out_shape=jax.ShapeDtypeStruct((AS, 2 * TOK + EXTRA, columns), BF16),
        in_specs=[in_hbm()] * 5,
        out_specs=in_vmem(),
        scratch_shapes=[
            pltpu.VMEM((TOK, AS * columns), BF16),
            pltpu.VMEM(lse.shape, F32),
            pltpu.VMEM(block_keep.shape, i32),
            pltpu.VMEM((8, ROWS), F32),
            dma((3, AS)),
            dma((2,)),
        ],
        compiler_params=pltpu.CompilerParams(vmem_limit_bytes=8 * 2**20),
        cost_estimate=pl.CostEstimate(flops=67108864, bytes_accessed=2800000, transcendentals=0),
    )(*held_in_hbm(query, out_grad, output, lse, block_keep))
    message = exchange(message_send)

    pieces = {0: kv_own}
    for off in (1, -1, 2, -2):
        pieces[off] = along_z(kv_own, off)
    pieces[3] = along_z(pieces[2], 1)
    pieces[-3] = along_z(pieces[-2], -1)
    pieces[4] = along_z(pieces[2], 2)

    keep = message[:, 2 * TOK + 4, :reach].astype(i32)
    ends = jnp.arange(doc_lengths.shape[0], dtype=i32)
    starts = jnp.sum(jnp.where(ends[None, :] < ends[:, None], doc_lengths[None, :], 0), axis=1)
    base = lax.axis_index("y").astype(i32) * WINDOW
    positions = (
        base
        + jnp.arange(AS, dtype=i32)[:, None] * CHUNK
        + z * TOK
        + (jnp.arange(ROWS, dtype=i32) % TOK)[None, :]
    )
    start_of = jnp.max(
        jnp.where(starts[None, None, :] <= positions[:, :, None], starts[None, None, :], 0), axis=2
    )
    start_of = jnp.maximum(start_of - base, 0)
    span = jnp.stack([start_of[:, 0], start_of[:, TOK - 1]], axis=1)

    scalars, start = (keep, span), start_of.reshape(AS, 1, ROWS)
    dqt, part = attention(FAR, scalars, message, start, pieces)
    from_three, from_four = along_z(part[3], -1), along_z(part[4], -2)
    from_minus_three = along_z(part[-3], 1)
    dq, near_part = attention(NEAR, scalars, message, start, pieces, dqt)
    part.update(near_part)
    one, minus_one = along_z(part[1], -1), along_z(part[-1], 1)
    two = along_z(partial_sum(part[2], from_three, from_four), -2)
    minus_two = along_z(partial_sum(part[-2], from_minus_three), 2)
    gradients = pl.pallas_call(
        pack_gradients_kernel,
        out_shape=[jax.ShapeDtypeStruct((TOK + 8, columns), BF16)] * AS,
        in_specs=[in_vmem()] * 6,
        out_specs=[in_vmem()] * AS,
        scratch_shapes=[pltpu.VMEM((AS, TOK, 2 * HD), BF16), dma((AS,))],
        compiler_params=small_kernel,
        cost_estimate=pl.CostEstimate(flops=400000, bytes_accessed=1900000, transcendentals=0),
    )(dq, part[0], one, minus_one, two, minus_two)
    gradients = [gradients[0]] + [shifted(gradients[k], k) for k in range(1, AS)]
    half = jax.ShapeDtypeStruct((TOK, KVH * HD), BF16)
    return pl.pallas_call(
        unpack_gradients_kernel,
        out_shape=[jax.ShapeDtypeStruct((TOK, AS * columns), BF16), half, half],
        in_specs=[in_vmem()] * AS,
        out_specs=[in_hbm()] * 3,
        scratch_shapes=[
            pltpu.VMEM(half.shape, BF16),
            pltpu.VMEM(half.shape, BF16),
            dma((AS + 2,)),
        ],
        compiler_params=small_kernel,
        cost_estimate=pl.CostEstimate(flops=0, bytes_accessed=1300000, transcendentals=0),
    )(*gradients)


def solution(mesh):
    fine = Mesh(mesh.devices.reshape(4, 2, 2, 2, ZS), ("y", "xl", "c", "xh", "z"))
    tokens = P(("y", "xl", "c", "xh", "z"), None)
    in_specs = (tokens,) * 6 + (P(), P(("y", "xl", "c"), None))
    return jax.shard_map(
        shards, mesh=fine, in_specs=in_specs, out_specs=(tokens,) * 3, check_vma=False
    )
```

```python
import functools
import math

import jax
import jax.numpy as jnp
from jax import lax
from jax.experimental import pallas as pl
from jax.experimental.pallas import tpu as pltpu
from jax.sharding import Mesh
from jax.sharding import PartitionSpec as P

KVH = 8
HD = 128
GROUP = 8
BLOCK = 128
WINDOW = 2048
TOK = 32
ZS = 8
AS = 8
CHUNK = TOK * ZS
ROWS = TOK * GROUP
SCALE = 1.0 / math.sqrt(HD)
LOG2E = math.log2(math.e)
BIG = 1e30
PAIR = 2
SPAN = 4
EXTRA = 8
HEADS = ("xl", "c", "xh")
F32 = jnp.float32
BF16 = jnp.bfloat16
EARLY = (1, -1)
FAR = (3, -3, 4)
LATE = (0, 2, -2)


def along_z(value, by):
    return lax.ppermute(value, "z", [(i, (i + by) % ZS) for i in range(ZS)])


def exchange(value):
    return lax.all_to_all(value, HEADS, split_axis=0, concat_axis=0, tiled=True)


def own_place():
    return (lax.axis_index("xl") * 2 + lax.axis_index("c")) * 2 + lax.axis_index("xh")


def shifted(value, by):
    return lax.ppermute(value, HEADS, [(i, (i + by) % AS) for i in range(AS)])


def pack_kv_kernel(k_hbm, v_hbm, out_ref, k_ref, v_ref, sems):
    copies = [
        pltpu.make_async_copy(k_hbm, k_ref, sems.at[0]),
        pltpu.make_async_copy(v_hbm, v_ref, sems.at[1]),
    ]
    for copy in copies:
        copy.start()
    for n, (copy, ref) in enumerate(zip(copies, (k_ref, v_ref))):
        copy.wait()
        for a in range(AS):
            out_ref[a, :, n * HD : (n + 1) * HD] = ref[:, a * HD : (a + 1) * HD]


def split(value):
    high = value.astype(BF16)
    return high, (value - high.astype(F32)).astype(BF16)


def pack_queries_kernel(
    q_hbm, g_hbm, o_hbm, lse_hbm, keep_hbm, out_ref, o_ref, lse_ref, keep_ref, row_ref, sems, small
):
    wide = GROUP * HD
    copies = [[], []]
    small_copies = [
        pltpu.make_async_copy(lse_hbm, lse_ref, small.at[0]),
        pltpu.make_async_copy(keep_hbm, keep_ref, small.at[1]),
    ]
    for copy in small_copies:
        copy.start()
    for a in range(AS):
        columns = pl.ds(a * wide, wide)
        for n, (src, dst) in enumerate(
            (
                (g_hbm, out_ref.at[a, pl.ds(TOK, TOK), :]),
                (o_hbm, o_ref.at[:, columns]),
            )
        ):
            copies[0].append(pltpu.make_async_copy(src.at[:, columns], dst, sems.at[n, a]))
        copies[1].append(
            pltpu.make_async_copy(
                q_hbm.at[:, columns], out_ref.at[a, pl.ds(0, TOK), :], sems.at[2, a]
            )
        )
    for copy in copies[0] + copies[1]:
        copy.start()
    ones = jnp.ones((EXTRA, 2 * HD), BF16)
    lane = lax.broadcasted_iota(jnp.int32, (TOK, ROWS), 1)
    spread = (lane % TOK == lax.broadcasted_iota(jnp.int32, (TOK, ROWS), 0)).astype(F32).astype(BF16)
    head_lane = lax.broadcasted_iota(jnp.int32, (GROUP, ROWS), 1) // TOK
    own_head = head_lane == lax.broadcasted_iota(jnp.int32, (GROUP, ROWS), 0)
    row = lax.broadcasted_iota(jnp.int32, (EXTRA, ROWS), 0)
    for copy in small_copies:
        copy.wait()
    place = lax.axis_index("xh") * 2 + lax.axis_index("z") // 4
    kept = keep_ref[...].astype(F32)
    at_place = lax.broadcasted_iota(jnp.int32, kept.shape, 0) == place
    row_ref[...] = jnp.zeros(row_ref.shape, F32)
    row_ref[0:1, : kept.shape[1]] = jnp.sum(jnp.where(at_place, kept, 0.0), axis=0, keepdims=True)
    flags = row_ref[0:1]
    scaled = lse_ref[...].T * LOG2E
    high, low = split(scaled)
    lower = split(scaled - high.astype(F32) - low.astype(F32))[0]
    lse_all = sum(jnp.dot(p, spread, preferred_element_type=F32) for p in (high, low, lower))
    for a in range(AS):
        copies[0][2 * a].wait()
        copies[0][2 * a + 1].wait()
        columns = slice(a * wide, (a + 1) * wide)
        product = out_ref[a, TOK : 2 * TOK, :].astype(F32) * o_ref[:, columns].astype(F32)
        high, low = split(product)
        stacked = jnp.concatenate(
            [
                jnp.concatenate([p[:, h * HD : (h + 1) * HD] for h in range(GROUP)], axis=0)
                for p in (high, low)
            ],
            axis=1,
        )
        delta = lax.dot_general(
            ones, stacked, (((1,), (1,)), ((), ())), preferred_element_type=F32
        )[:1]
        lse = jnp.sum(
            jnp.where(own_head, lse_all[a * GROUP : (a + 1) * GROUP], 0.0), axis=0, keepdims=True
        )
        lse_high, lse_low = split(lse)
        delta_high, delta_low = split(delta)
        extra = jnp.zeros((EXTRA, ROWS), F32)
        for n, part in enumerate((lse_high, lse_low, delta_high, delta_low, flags)):
            extra = jnp.where(row == n, part.astype(F32), extra)
        out_ref[a, 2 * TOK :, :ROWS] = extra.astype(BF16)
        out_ref[a, 2 * TOK :, ROWS:] = jnp.zeros((EXTRA, wide - ROWS), BF16)
    for copy in copies[1]:
        copy.wait()


def attention_kernel(offsets, first_call, final, keep_ref, message_ref, start_ref, *refs):
    pieces = len(offsets)
    kv_refs, refs = refs[:pieces], refs[pieces:]
    if not first_call:
        dqt_in_ref, refs = refs[0], refs[1:]
    dq_ref, refs = refs[0], refs[1:]
    dkv_refs, refs = refs[:pieces], refs[pieces:]
    acc_ref, kt_ref, q_ref, g_ref, qt_ref, gt_ref, dqt_ref = refs
    z = lax.axis_index("z")
    sources = [lax.rem(z - off + ZS, ZS) for off in offsets]
    halves = [source // 4 for source in sources]
    lane_token = lax.rem(lax.broadcasted_iota(jnp.int32, (1, ROWS), 1), TOK)
    sublane = lax.broadcasted_iota(jnp.int32, (TOK, ROWS), 0)
    keys = SPAN * pieces * TOK

    def keys_of(b, lanes):
        return jnp.concatenate(
            [kv[b * SPAN + c, :, lanes] for c in range(SPAN) for kv in kv_refs], axis=0
        )

    for b in range(AS // SPAN):
        kt_ref[b] = keys_of(b, pl.ds(0, HD)).T

    def load(j, slot):
        vectors = []
        for c in range(PAIR):
            i = j * PAIR + c
            for h in range(GROUP):
                rows = pl.ds(c * ROWS + h * TOK, TOK)
                q_ref[slot, rows, :] = message_ref[i, :TOK, h * HD : (h + 1) * HD]
                g_ref[slot, rows, :] = message_ref[i, TOK : 2 * TOK, h * HD : (h + 1) * HD]
            extra = message_ref[i, 2 * TOK :, :ROWS].astype(F32)
            q_pos = i * CHUNK + z * TOK + lane_token
            vectors.append((extra[0:1] + extra[1:2], extra[2:3] + extra[3:4], start_ref[i], q_pos))
        qt_ref[slot] = q_ref[slot].T
        gt_ref[slot] = g_ref[slot].T
        return vectors

    def tile(j, b, slot, vectors):
        reaches_own = (b + 1) * SPAN > j * PAIR
        scores = jnp.dot(keys_of(b, pl.ds(0, HD)), qt_ref[slot], preferred_element_type=F32)
        dprobs = jnp.dot(keys_of(b, pl.ds(HD, HD)), gt_ref[slot], preferred_element_type=F32)
        probs_b, dscores_b = [], []
        for k in range(SPAN * pieces):
            a, r = b * SPAN + k // pieces, k % pieces
            rows = slice(k * TOK, (k + 1) * TOK)
            probs_row, dscores_row = [], []
            for c, (lse, delta, start, q_pos) in enumerate(vectors):
                i = j * PAIR + c
                columns = slice(c * ROWS, (c + 1) * ROWS)
                distance = 2 * (i - a) + z // 4 - halves[r]
                kept = keep_ref[i, jnp.maximum(distance, 0)] > 0
                shift = lse + jnp.where(kept, 0.0, BIG)
                probs = jnp.exp2(scores[rows, columns] * (SCALE * LOG2E) - shift)
                k_pos = a * CHUNK + sources[r] * TOK + sublane
                allowed = k_pos >= start
                if reaches_own:
                    allowed = allowed & (k_pos <= q_pos)
                probs = jnp.where(allowed, probs, 0.0)
                probs_row.append(probs.astype(BF16))
                dscores_row.append((probs * (dprobs[rows, columns] - delta)).astype(BF16))
            probs_b.append(jnp.concatenate(probs_row, axis=1))
            dscores_b.append(jnp.concatenate(dscores_row, axis=1))
        probs_b = jnp.concatenate(probs_b, axis=0)
        dscores_b = jnp.concatenate(dscores_b, axis=0)
        dk = jnp.dot(dscores_b, q_ref[slot], preferred_element_type=F32)
        dv = jnp.dot(probs_b, g_ref[slot], preferred_element_type=F32)
        if j == b * SPAN // PAIR:
            acc_ref[b, :, :HD] = dk
            acc_ref[b, :, HD:] = dv
        else:
            acc_ref[b, :, :HD] += dk
            acc_ref[b, :, HD:] += dv
        dq = jnp.dot(kt_ref[b], dscores_b, preferred_element_type=F32)
        if b == 0 and first_call:
            dqt_ref[slot] = dq
        elif b == 0:
            dqt_ref[slot] = dqt_in_ref[j] + dq
        else:
            dqt_ref[slot] += dq

    for j in range(AS // PAIR):
        slot = j % 2
        vectors = load(j, slot)
        for b in range(j * PAIR // SPAN + 1):
            tile(j, b, slot, vectors)
        if not final:
            dq_ref[j] = dqt_ref[slot]
            continue
        dq = (dqt_ref[slot] * SCALE).T.astype(BF16)
        for c in range(PAIR):
            for h in range(GROUP):
                at = c * ROWS + h * TOK
                dq_ref[j * PAIR + c, :, h * HD : (h + 1) * HD] = dq[at : at + TOK]

    for b in range(AS // SPAN):
        for k in range(SPAN * pieces):
            piece = acc_ref[b, k * TOK : (k + 1) * TOK, :]
            out = dkv_refs[k % pieces].at[b * SPAN + k // pieces]
            out[:, :HD] = (piece[:, :HD] * SCALE).astype(BF16)
            out[:, HD:] = piece[:, HD:].astype(BF16)


def attention(offsets, keep, message, start, kv, dqt=None, final=False):
    first_call = dqt is None
    pieces = len(offsets)
    keys = SPAN * pieces * TOK
    rows = PAIR * ROWS
    dqt_shape = jax.ShapeDtypeStruct((AS // PAIR, HD, rows), F32)
    dq_shape = jax.ShapeDtypeStruct((AS, TOK, GROUP * HD), BF16)
    results = pl.pallas_call(
        functools.partial(attention_kernel, offsets, first_call, final),
        out_shape=[dq_shape if final else dqt_shape]
        + [jax.ShapeDtypeStruct((AS, TOK, 2 * HD), BF16)] * pieces,
        in_specs=[in_smem()] + [in_vmem()] * (2 + pieces + (not first_call)),
        out_specs=[in_vmem()] * (1 + pieces),
        scratch_shapes=[
            pltpu.VMEM((AS // SPAN, keys, 2 * HD), F32),
            pltpu.VMEM((AS // SPAN, HD, keys), BF16),
            pltpu.VMEM((2, rows, HD), BF16),
            pltpu.VMEM((2, rows, HD), BF16),
            pltpu.VMEM((2, HD, rows), BF16),
            pltpu.VMEM((2, HD, rows), BF16),
            pltpu.VMEM((2, HD, rows), F32),
        ],
        compiler_params=pltpu.CompilerParams(vmem_limit_bytes=24 * 2**20),
        cost_estimate=pl.CostEstimate(
            flops=400000000 * pieces, bytes_accessed=3000000, transcendentals=300000 * pieces
        ),
    )(keep, message, start, *[kv[o] for o in offsets], *([] if first_call else [dqt]))
    return results[0], dict(zip(offsets, results[1:]))


def sum_kernel(*refs):
    total = refs[0][...].astype(F32)
    for ref in refs[1:-1]:
        total = total + ref[...].astype(F32)
    refs[-1][...] = total.astype(BF16)


def pack_gradients_kernel(dq_ref, *refs):
    pieces, out_refs, (total_ref, sems) = refs[:5], refs[5 : 5 + AS], refs[5 + AS :]
    me = own_place()
    copies = []
    for k, out_ref in enumerate(out_refs):
        there = lax.rem(me + k, AS)
        copies.append(
            pltpu.make_async_copy(dq_ref.at[there], out_ref.at[pl.ds(0, TOK), :], sems.at[k])
        )
    for copy in copies:
        copy.start()
    total = pieces[0][...].astype(F32)
    for piece in pieces[1:]:
        total = total + piece[...].astype(F32)
    total_ref[...] = total.astype(BF16)
    for k, out_ref in enumerate(out_refs):
        there = lax.rem(me + k, AS)
        for n in range(TOK // 8):
            columns = slice(n * 2 * HD, (n + 1) * 2 * HD)
            out_ref[TOK:, columns] = total_ref[there, n * 8 : (n + 1) * 8, :]
    for copy in copies:
        copy.wait()


def unpack_gradients_kernel(*refs):
    in_refs, (dq_hbm, dk_hbm, dv_hbm, dk_ref, dv_ref, sems) = refs[:AS], refs[AS:]
    wide = GROUP * HD
    me = own_place()
    copies = []
    for k, in_ref in enumerate(in_refs):
        a = lax.rem(me - k + AS, AS)
        columns = pl.ds(pl.multiple_of(a * wide, wide), wide)
        copies.append(
            pltpu.make_async_copy(in_ref.at[pl.ds(0, TOK), :], dq_hbm.at[:, columns], sems.at[k])
        )
        copies[-1].start()
    for k, in_ref in enumerate(in_refs):
        a = lax.rem(me - k + AS, AS)
        columns = pl.ds(pl.multiple_of(a * HD, HD), HD)
        for n in range(TOK // 8):
            rows = slice(n * 8, (n + 1) * 8)
            dk_ref[rows, columns] = in_ref[TOK:, 2 * n * HD : (2 * n + 1) * HD]
            dv_ref[rows, columns] = in_ref[TOK:, (2 * n + 1) * HD : (2 * n + 2) * HD]
    copies.append(pltpu.make_async_copy(dk_ref, dk_hbm, sems.at[AS]))
    copies.append(pltpu.make_async_copy(dv_ref, dv_hbm, sems.at[AS + 1]))
    copies[-2].start()
    copies[-1].start()
    for copy in copies:
        copy.wait()


def in_hbm():
    return pl.BlockSpec(memory_space=pltpu.HBM)


def held_in_hbm(*values):
    return [pltpu.with_memory_space_constraint(v, pltpu.HBM) for v in values]


def anywhere():
    return pl.BlockSpec(memory_space=pl.ANY)


def in_vmem():
    return pl.BlockSpec(memory_space=pltpu.VMEM)


def in_smem():
    return pl.BlockSpec(memory_space=pltpu.SMEM)


def partial_sum(*values):
    shape = values[0].shape
    return pl.pallas_call(
        sum_kernel,
        out_shape=jax.ShapeDtypeStruct(shape, BF16),
        in_specs=[in_vmem()] * len(values),
        out_specs=in_vmem(),
        compiler_params=pltpu.CompilerParams(vmem_limit_bytes=4 * 2**20),
        cost_estimate=pl.CostEstimate(
            flops=65536 * len(values), bytes_accessed=131072 * (1 + len(values)), transcendentals=0
        ),
    )(*values)


def shards(query, key, value, output, out_grad, lse, doc_lengths, block_keep):
    i32 = jnp.int32
    z = lax.axis_index("z").astype(i32)
    columns = GROUP * HD
    dma = pltpu.SemaphoreType.DMA
    small_kernel = pltpu.CompilerParams(vmem_limit_bytes=4 * 2**20)

    kv_send = pl.pallas_call(
        pack_kv_kernel,
        out_shape=jax.ShapeDtypeStruct((AS, TOK, 2 * HD), BF16),
        in_specs=[in_hbm(), in_hbm()],
        out_specs=in_vmem(),
        scratch_shapes=[pltpu.VMEM(key.shape, BF16), pltpu.VMEM(key.shape, BF16), dma((2,))],
        compiler_params=small_kernel,
        cost_estimate=pl.CostEstimate(flops=0, bytes_accessed=262144, transcendentals=0),
    )(*held_in_hbm(key, value))
    kv_own = exchange(kv_send)

    reach = block_keep.shape[1]
    message_send = pl.pallas_call(
        pack_queries_kernel,
        out_shape=jax.ShapeDtypeStruct((AS, 2 * TOK + EXTRA, columns), BF16),
        in_specs=[in_hbm()] * 5,
        out_specs=in_vmem(),
        scratch_shapes=[
            pltpu.VMEM((TOK, AS * columns), BF16),
            pltpu.VMEM(lse.shape, F32),
            pltpu.VMEM(block_keep.shape, i32),
            pltpu.VMEM((8, ROWS), F32),
            dma((3, AS)),
            dma((2,)),
        ],
        compiler_params=pltpu.CompilerParams(vmem_limit_bytes=8 * 2**20),
        cost_estimate=pl.CostEstimate(flops=67108864, bytes_accessed=2800000, transcendentals=0),
    )(*held_in_hbm(query, out_grad, output, lse, block_keep))
    message = exchange(message_send)

    pieces = {0: kv_own}
    for off in (1, -1, 2, -2):
        pieces[off] = along_z(kv_own, off)
    pieces[3] = along_z(pieces[2], 1)
    pieces[-3] = along_z(pieces[-2], -1)
    pieces[4] = along_z(pieces[2], 2)

    keep = message[:, 2 * TOK + 4, :reach].astype(i32)
    ends = jnp.arange(doc_lengths.shape[0], dtype=i32)
    starts = jnp.sum(jnp.where(ends[None, :] < ends[:, None], doc_lengths[None, :], 0), axis=1)
    base = lax.axis_index("y").astype(i32) * WINDOW
    positions = (
        base
        + jnp.arange(AS, dtype=i32)[:, None] * CHUNK
        + z * TOK
        + (jnp.arange(ROWS, dtype=i32) % TOK)[None, :]
    )
    start_of = jnp.max(
        jnp.where(starts[None, None, :] <= positions[:, :, None], starts[None, None, :], 0), axis=2
    )
    start_of = jnp.maximum(start_of - base, 0)

    start = start_of.reshape(AS, 1, ROWS)
    dqt, part = attention(EARLY, keep, message, start, pieces)
    one, minus_one = along_z(part[1], -1), along_z(part[-1], 1)
    dqt, far_part = attention(FAR, keep, message, start, pieces, dqt)
    from_three, from_four = along_z(far_part[3], -1), along_z(far_part[4], -2)
    from_minus_three = along_z(far_part[-3], 1)
    dq, part = attention(LATE, keep, message, start, pieces, dqt, final=True)
    two = along_z(partial_sum(part[2], from_three, from_four), -2)
    minus_two = along_z(partial_sum(part[-2], from_minus_three), 2)
    gradients = pl.pallas_call(
        pack_gradients_kernel,
        out_shape=[jax.ShapeDtypeStruct((TOK + 8, columns), BF16)] * AS,
        in_specs=[in_vmem()] * 6,
        out_specs=[in_vmem()] * AS,
        scratch_shapes=[pltpu.VMEM((AS, TOK, 2 * HD), BF16), dma((AS,))],
        compiler_params=small_kernel,
        cost_estimate=pl.CostEstimate(flops=400000, bytes_accessed=1900000, transcendentals=0),
    )(dq, part[0], one, minus_one, two, minus_two)
    gradients = [gradients[0]] + [shifted(gradients[k], k) for k in range(1, AS)]
    half = jax.ShapeDtypeStruct((TOK, KVH * HD), BF16)
    return pl.pallas_call(
        unpack_gradients_kernel,
        out_shape=[jax.ShapeDtypeStruct((TOK, AS * columns), BF16), half, half],
        in_specs=[in_vmem()] * AS,
        out_specs=[in_hbm()] * 3,
        scratch_shapes=[
            pltpu.VMEM(half.shape, BF16),
            pltpu.VMEM(half.shape, BF16),
            dma((AS + 2,)),
        ],
        compiler_params=small_kernel,
        cost_estimate=pl.CostEstimate(flops=0, bytes_accessed=1300000, transcendentals=0),
    )(*gradients)


def solution(mesh):
    fine = Mesh(mesh.devices.reshape(4, 2, 2, 2, ZS), ("y", "xl", "c", "xh", "z"))
    tokens = P(("y", "xl", "c", "xh", "z"), None)
    in_specs = (tokens,) * 6 + (P(), P(("y", "xl", "c"), None))
    return jax.shard_map(
        shards, mesh=fine, in_specs=in_specs, out_specs=(tokens,) * 3, check_vma=False
    )
```

```python
import functools
import math

import jax
import jax.numpy as jnp
from jax import lax
from jax.experimental import pallas as pl
from jax.experimental.pallas import tpu as pltpu
from jax.sharding import Mesh
from jax.sharding import PartitionSpec as P

KVH = 8
HD = 128
GROUP = 8
BLOCK = 128
WINDOW = 2048
TOK = 32
ZS = 8
AS = 8
CHUNK = TOK * ZS
ROWS = TOK * GROUP
SCALE = 1.0 / math.sqrt(HD)
LOG2E = math.log2(math.e)
BIG = 1e30
PAIR = 2
SPAN = 4
EXTRA = 16
HEADS = ("xl", "c", "xh")
F32 = jnp.float32
BF16 = jnp.bfloat16
EARLY = (1, -1)
FAR = (3, -3, 4)
LATE = (0, 2, -2)


def along_z(value, by):
    return lax.ppermute(value, "z", [(i, (i + by) % ZS) for i in range(ZS)])


def exchange(value):
    return lax.all_to_all(value, HEADS, split_axis=0, concat_axis=0, tiled=True)


def own_place():
    return (lax.axis_index("xl") * 2 + lax.axis_index("c")) * 2 + lax.axis_index("xh")


def shifted(value, by):
    return lax.ppermute(value, HEADS, [(i, (i + by) % AS) for i in range(AS)])


def pack_kv_kernel(k_hbm, v_hbm, out_ref, k_ref, v_ref, sems):
    copies = [
        pltpu.make_async_copy(k_hbm, k_ref, sems.at[0]),
        pltpu.make_async_copy(v_hbm, v_ref, sems.at[1]),
    ]
    for copy in copies:
        copy.start()
    for n, (copy, ref) in enumerate(zip(copies, (k_ref, v_ref))):
        copy.wait()
        for a in range(AS):
            out_ref[a, :, n * HD : (n + 1) * HD] = ref[:, a * HD : (a + 1) * HD]


def split(value):
    high = value.astype(BF16)
    return high, (value - high.astype(F32)).astype(BF16)


def pack_queries_kernel(q_hbm, g_hbm, o_hbm, lse_hbm, keep_hbm, out_ref, *refs):
    q_ref, g_ref, o_ref, lse_ref, keep_ref, row_ref, sems, small = refs
    wide = GROUP * HD
    small_copies = [
        pltpu.make_async_copy(lse_hbm, lse_ref, small.at[0]),
        pltpu.make_async_copy(keep_hbm, keep_ref, small.at[1]),
    ]
    for copy in small_copies:
        copy.start()
    copies = []
    for a in range(AS):
        columns = pl.ds(a * wide, wide)
        copies.append(
            [
                pltpu.make_async_copy(src.at[:, columns], dst.at[:, columns], sems.at[n, a])
                for n, (src, dst) in enumerate(((g_hbm, g_ref), (o_hbm, o_ref), (q_hbm, q_ref)))
            ]
        )
        for copy in copies[a]:
            copy.start()
    ones = jnp.ones((8, 2 * HD), BF16)
    lane = lax.broadcasted_iota(jnp.int32, (TOK, ROWS), 1)
    spread = (lane % TOK == lax.broadcasted_iota(jnp.int32, (TOK, ROWS), 0)).astype(F32).astype(BF16)
    head_lane = lax.broadcasted_iota(jnp.int32, (GROUP, ROWS), 1) // TOK
    own_head = head_lane == lax.broadcasted_iota(jnp.int32, (GROUP, ROWS), 0)
    row = lax.broadcasted_iota(jnp.int32, (EXTRA, HD), 0)
    for copy in small_copies:
        copy.wait()
    place = lax.axis_index("xh") * 2 + lax.axis_index("z") // 4
    kept = keep_ref[...].astype(F32)
    at_place = lax.broadcasted_iota(jnp.int32, kept.shape, 0) == place
    row_ref[...] = jnp.zeros(row_ref.shape, F32)
    row_ref[0:1, : kept.shape[1]] = jnp.sum(jnp.where(at_place, kept, 0.0), axis=0, keepdims=True)
    flags = row_ref[0:1]
    scaled = lse_ref[...].T * LOG2E
    high, low = split(scaled)
    lower = split(scaled - high.astype(F32) - low.astype(F32))[0]
    lse_all = sum(jnp.dot(p, spread, preferred_element_type=F32) for p in (high, low, lower))
    for a in range(AS):
        for copy in copies[a]:
            copy.wait()
        columns = slice(a * wide, (a + 1) * wide)
        for h in range(GROUP):
            head = slice((a * GROUP + h) * HD, (a * GROUP + h + 1) * HD)
            out_ref[a, h * TOK : (h + 1) * TOK, :] = q_ref[:, head]
            out_ref[a, ROWS + h * TOK : ROWS + (h + 1) * TOK, :] = g_ref[:, head]
        product = g_ref[:, columns].astype(F32) * o_ref[:, columns].astype(F32)
        high, low = split(product)
        stacked = jnp.concatenate(
            [
                jnp.concatenate([p[:, h * HD : (h + 1) * HD] for h in range(GROUP)], axis=0)
                for p in (high, low)
            ],
            axis=1,
        )
        delta = lax.dot_general(
            ones, stacked, (((1,), (1,)), ((), ())), preferred_element_type=F32
        )[:1]
        lse = jnp.sum(
            jnp.where(own_head, lse_all[a * GROUP : (a + 1) * GROUP], 0.0), axis=0, keepdims=True
        )
        parts = [p.astype(F32) for p in split(lse) + split(delta)]
        extra = jnp.where(row == 8, flags, 0.0)
        for n, part in enumerate(parts):
            extra = jnp.where(row == 2 * n, part[:, :HD], extra)
            extra = jnp.where(row == 2 * n + 1, part[:, HD:], extra)
        out_ref[a, 2 * ROWS :, :] = extra.astype(BF16)


def attention_kernel(offsets, first_call, final, keep_ref, message_ref, start_ref, *refs):
    pieces = len(offsets)
    kv_refs, refs = refs[:pieces], refs[pieces:]
    if not first_call:
        dqt_in_ref, refs = refs[0], refs[1:]
    dq_ref, refs = refs[0], refs[1:]
    dkv_refs, refs = refs[:pieces], refs[pieces:]
    acc_ref, kt_ref, qt_ref, gt_ref, dqt_ref = refs
    z = lax.axis_index("z")
    sources = [lax.rem(z - off + ZS, ZS) for off in offsets]
    halves = [source // 4 for source in sources]
    lane_token = lax.rem(lax.broadcasted_iota(jnp.int32, (1, ROWS), 1), TOK)
    sublane = lax.broadcasted_iota(jnp.int32, (TOK, ROWS), 0)
    keys = SPAN * pieces * TOK

    def keys_of(b, lanes):
        return jnp.concatenate(
            [kv[b * SPAN + c, :, lanes] for c in range(SPAN) for kv in kv_refs], axis=0
        )

    for b in range(AS // SPAN):
        kt_ref[b] = keys_of(b, pl.ds(0, HD)).T

    def rows_of(j, first):
        return jnp.concatenate(
            [message_ref[j * PAIR + c, first : first + ROWS, :] for c in range(PAIR)], axis=0
        )

    def load(j, slot):
        vectors = []
        for c in range(PAIR):
            i = j * PAIR + c
            extra = message_ref[i, 2 * ROWS :, :].astype(F32)
            summed = [extra[n : n + 1] + extra[n + 2 : n + 3] for n in (0, 1, 4, 5)]
            lse = jnp.concatenate(summed[:2], axis=1)
            delta = jnp.concatenate(summed[2:], axis=1)
            vectors.append((lse, delta, start_ref[i], i * CHUNK + z * TOK + lane_token))
        qt_ref[slot] = rows_of(j, 0).T
        gt_ref[slot] = rows_of(j, ROWS).T
        return vectors

    def tile(j, b, slot, vectors):
        reaches_own = (b + 1) * SPAN > j * PAIR
        scores = jnp.dot(keys_of(b, pl.ds(0, HD)), qt_ref[slot], preferred_element_type=F32)
        dprobs = jnp.dot(keys_of(b, pl.ds(HD, HD)), gt_ref[slot], preferred_element_type=F32)
        probs_b, dscores_b = [], []
        for k in range(SPAN * pieces):
            a, r = b * SPAN + k // pieces, k % pieces
            rows = slice(k * TOK, (k + 1) * TOK)
            probs_row, dscores_row = [], []
            for c, (lse, delta, start, q_pos) in enumerate(vectors):
                i = j * PAIR + c
                columns = slice(c * ROWS, (c + 1) * ROWS)
                distance = 2 * (i - a) + z // 4 - halves[r]
                kept = keep_ref[i, jnp.maximum(distance, 0)] > 0
                shift = lse + jnp.where(kept, 0.0, BIG)
                probs = jnp.exp2(scores[rows, columns] * (SCALE * LOG2E) - shift)
                k_pos = a * CHUNK + sources[r] * TOK + sublane
                allowed = k_pos >= start
                if reaches_own:
                    allowed = allowed & (k_pos <= q_pos)
                probs = jnp.where(allowed, probs, 0.0)
                probs_row.append(probs.astype(BF16))
                dscores_row.append((probs * (dprobs[rows, columns] - delta)).astype(BF16))
            probs_b.append(jnp.concatenate(probs_row, axis=1))
            dscores_b.append(jnp.concatenate(dscores_row, axis=1))
        probs_b = jnp.concatenate(probs_b, axis=0)
        dscores_b = jnp.concatenate(dscores_b, axis=0)
        dk = jnp.dot(dscores_b, rows_of(j, 0), preferred_element_type=F32)
        dv = jnp.dot(probs_b, rows_of(j, ROWS), preferred_element_type=F32)
        if j == b * SPAN // PAIR:
            acc_ref[b, :, :HD] = dk
            acc_ref[b, :, HD:] = dv
        else:
            acc_ref[b, :, :HD] += dk
            acc_ref[b, :, HD:] += dv
        dq = jnp.dot(kt_ref[b], dscores_b, preferred_element_type=F32)
        if b == 0 and first_call:
            dqt_ref[slot] = dq
        elif b == 0:
            dqt_ref[slot] = dqt_in_ref[j] + dq
        else:
            dqt_ref[slot] += dq

    for j in range(AS // PAIR):
        slot = j % 2
        vectors = load(j, slot)
        for b in range(j * PAIR // SPAN + 1):
            tile(j, b, slot, vectors)
        if not final:
            dq_ref[j] = dqt_ref[slot]
            continue
        dq = (dqt_ref[slot] * SCALE).T.astype(BF16)
        for c in range(PAIR):
            for h in range(GROUP):
                at = c * ROWS + h * TOK
                dq_ref[j * PAIR + c, :, h * HD : (h + 1) * HD] = dq[at : at + TOK]

    for b in range(AS // SPAN):
        for k in range(SPAN * pieces):
            piece = acc_ref[b, k * TOK : (k + 1) * TOK, :]
            out = dkv_refs[k % pieces].at[b * SPAN + k // pieces]
            out[:, :HD] = (piece[:, :HD] * SCALE).astype(BF16)
            out[:, HD:] = piece[:, HD:].astype(BF16)


def attention(offsets, keep, message, start, kv, dqt=None, final=False):
    first_call = dqt is None
    pieces = len(offsets)
    keys = SPAN * pieces * TOK
    rows = PAIR * ROWS
    dqt_shape = jax.ShapeDtypeStruct((AS // PAIR, HD, rows), F32)
    dq_shape = jax.ShapeDtypeStruct((AS, TOK, GROUP * HD), BF16)
    results = pl.pallas_call(
        functools.partial(attention_kernel, offsets, first_call, final),
        out_shape=[dq_shape if final else dqt_shape]
        + [jax.ShapeDtypeStruct((AS, TOK, 2 * HD), BF16)] * pieces,
        in_specs=[in_smem()] + [in_vmem()] * (2 + pieces + (not first_call)),
        out_specs=[in_vmem()] * (1 + pieces),
        scratch_shapes=[
            pltpu.VMEM((AS // SPAN, keys, 2 * HD), F32),
            pltpu.VMEM((AS // SPAN, HD, keys), BF16),
            pltpu.VMEM((2, HD, rows), BF16),
            pltpu.VMEM((2, HD, rows), BF16),
            pltpu.VMEM((2, HD, rows), F32),
        ],
        compiler_params=pltpu.CompilerParams(vmem_limit_bytes=24 * 2**20),
        cost_estimate=pl.CostEstimate(
            flops=400000000 * pieces, bytes_accessed=3000000, transcendentals=300000 * pieces
        ),
    )(keep, message, start, *[kv[o] for o in offsets], *([] if first_call else [dqt]))
    return results[0], dict(zip(offsets, results[1:]))


def sum_kernel(*refs):
    total = refs[0][...].astype(F32)
    for ref in refs[1:-1]:
        total = total + ref[...].astype(F32)
    refs[-1][...] = total.astype(BF16)


def pack_gradients_kernel(*refs):
    pieces, out_refs, (total_ref,) = refs[:5], refs[5 : 5 + AS], refs[5 + AS :]
    me = own_place()
    total = pieces[0][...].astype(F32)
    for piece in pieces[1:]:
        total = total + piece[...].astype(F32)
    total_ref[...] = total.astype(BF16)
    for k, out_ref in enumerate(out_refs):
        there = lax.rem(me + k, AS)
        for n in range(TOK // 8):
            columns = slice(n * 2 * HD, (n + 1) * 2 * HD)
            out_ref[:, columns] = total_ref[there, n * 8 : (n + 1) * 8, :]


def unpack_queries_kernel(in_ref, out_hbm, sems):
    wide = GROUP * HD
    copies = [
        pltpu.make_async_copy(in_ref.at[a], out_hbm.at[:, pl.ds(a * wide, wide)], sems.at[a])
        for a in range(AS)
    ]
    for copy in copies:
        copy.start()
    for copy in copies:
        copy.wait()


def unpack_gradients_kernel(*refs):
    in_refs, (dk_ref, dv_ref) = refs[:AS], refs[AS:]
    me = own_place()
    for k, in_ref in enumerate(in_refs):
        a = lax.rem(me - k + AS, AS)
        columns = pl.ds(pl.multiple_of(a * HD, HD), HD)
        for n in range(TOK // 8):
            rows = slice(n * 8, (n + 1) * 8)
            dk_ref[rows, columns] = in_ref[:, 2 * n * HD : (2 * n + 1) * HD]
            dv_ref[rows, columns] = in_ref[:, (2 * n + 1) * HD : (2 * n + 2) * HD]


def in_hbm():
    return pl.BlockSpec(memory_space=pltpu.HBM)


def held_in_hbm(*values):
    return [pltpu.with_memory_space_constraint(v, pltpu.HBM) for v in values]


def anywhere():
    return pl.BlockSpec(memory_space=pl.ANY)


def in_vmem():
    return pl.BlockSpec(memory_space=pltpu.VMEM)


def in_smem():
    return pl.BlockSpec(memory_space=pltpu.SMEM)


def partial_sum(*values):
    shape = values[0].shape
    return pl.pallas_call(
        sum_kernel,
        out_shape=jax.ShapeDtypeStruct(shape, BF16),
        in_specs=[in_vmem()] * len(values),
        out_specs=in_vmem(),
        compiler_params=pltpu.CompilerParams(vmem_limit_bytes=4 * 2**20),
        cost_estimate=pl.CostEstimate(
            flops=65536 * len(values), bytes_accessed=131072 * (1 + len(values)), transcendentals=0
        ),
    )(*values)


def shards(query, key, value, output, out_grad, lse, doc_lengths, block_keep):
    i32 = jnp.int32
    z = lax.axis_index("z").astype(i32)
    columns = GROUP * HD
    dma = pltpu.SemaphoreType.DMA
    small_kernel = pltpu.CompilerParams(vmem_limit_bytes=4 * 2**20)

    kv_send = pl.pallas_call(
        pack_kv_kernel,
        out_shape=jax.ShapeDtypeStruct((AS, TOK, 2 * HD), BF16),
        in_specs=[in_hbm(), in_hbm()],
        out_specs=in_vmem(),
        scratch_shapes=[pltpu.VMEM(key.shape, BF16), pltpu.VMEM(key.shape, BF16), dma((2,))],
        compiler_params=small_kernel,
        cost_estimate=pl.CostEstimate(flops=0, bytes_accessed=262144, transcendentals=0),
    )(*held_in_hbm(key, value))
    kv_own = exchange(kv_send)

    reach = block_keep.shape[1]
    message_send = pl.pallas_call(
        pack_queries_kernel,
        out_shape=jax.ShapeDtypeStruct((AS, 2 * ROWS + EXTRA, HD), BF16),
        in_specs=[in_hbm()] * 5,
        out_specs=in_vmem(),
        scratch_shapes=[
            pltpu.VMEM((TOK, AS * columns), BF16),
            pltpu.VMEM((TOK, AS * columns), BF16),
            pltpu.VMEM((TOK, AS * columns), BF16),
            pltpu.VMEM(lse.shape, F32),
            pltpu.VMEM(block_keep.shape, i32),
            pltpu.VMEM((8, HD), F32),
            dma((3, AS)),
            dma((2,)),
        ],
        compiler_params=pltpu.CompilerParams(vmem_limit_bytes=8 * 2**20),
        cost_estimate=pl.CostEstimate(flops=67108864, bytes_accessed=2800000, transcendentals=0),
    )(*held_in_hbm(query, out_grad, output, lse, block_keep))
    message = exchange(message_send)

    pieces = {0: kv_own}
    for off in (1, -1, 2, -2):
        pieces[off] = along_z(kv_own, off)
    pieces[3] = along_z(pieces[2], 1)
    pieces[-3] = along_z(pieces[-2], -1)
    pieces[4] = along_z(pieces[2], 2)

    keep = message[:, 2 * ROWS + 8, :reach].astype(i32)
    ends = jnp.arange(doc_lengths.shape[0], dtype=i32)
    starts = jnp.sum(jnp.where(ends[None, :] < ends[:, None], doc_lengths[None, :], 0), axis=1)
    base = lax.axis_index("y").astype(i32) * WINDOW
    positions = (
        base
        + jnp.arange(AS, dtype=i32)[:, None] * CHUNK
        + z * TOK
        + (jnp.arange(ROWS, dtype=i32) % TOK)[None, :]
    )
    start_of = jnp.max(
        jnp.where(starts[None, None, :] <= positions[:, :, None], starts[None, None, :], 0), axis=2
    )
    start_of = jnp.maximum(start_of - base, 0)

    start = start_of.reshape(AS, 1, ROWS)
    dqt, part = attention(EARLY, keep, message, start, pieces)
    one, minus_one = along_z(part[1], -1), along_z(part[-1], 1)
    dqt, far_part = attention(FAR, keep, message, start, pieces, dqt)
    from_three, from_four = along_z(far_part[3], -1), along_z(far_part[4], -2)
    from_minus_three = along_z(far_part[-3], 1)
    dqt, one, minus_one = lax.optimization_barrier((dqt, one, minus_one))
    dq, late_part = attention(LATE, keep, message, start, pieces, dqt, final=True)
    two = along_z(partial_sum(late_part[2], from_three, from_four), -2)
    minus_two = along_z(partial_sum(late_part[-2], from_minus_three), 2)
    dq_back = exchange(dq)
    returned = (late_part[0], one, minus_one, two, minus_two)
    query_grad = pl.pallas_call(
        unpack_queries_kernel,
        out_shape=jax.ShapeDtypeStruct((TOK, AS * columns), BF16),
        in_specs=[in_vmem()],
        out_specs=in_hbm(),
        scratch_shapes=[dma((AS,))],
        compiler_params=small_kernel,
        cost_estimate=pl.CostEstimate(flops=0, bytes_accessed=1048576, transcendentals=0),
    )(dq_back)
    gradients = pl.pallas_call(
        pack_gradients_kernel,
        out_shape=[jax.ShapeDtypeStruct((8, columns), BF16)] * AS,
        in_specs=[in_vmem()] * 5,
        out_specs=[in_vmem()] * AS,
        scratch_shapes=[pltpu.VMEM((AS, TOK, 2 * HD), BF16)],
        compiler_params=small_kernel,
        cost_estimate=pl.CostEstimate(flops=5000000000, bytes_accessed=900000, transcendentals=0),
    )(*returned)
    gradients = [gradients[0]] + [shifted(gradients[k], k) for k in range(1, AS)]
    query_grad, gradients = lax.optimization_barrier((query_grad, gradients))
    half = jax.ShapeDtypeStruct((TOK, KVH * HD), BF16)
    key_grad, value_grad = pl.pallas_call(
        unpack_gradients_kernel,
        out_shape=[half, half],
        in_specs=[in_vmem()] * AS,
        out_specs=[in_vmem()] * 2,
        compiler_params=small_kernel,
        cost_estimate=pl.CostEstimate(flops=0, bytes_accessed=262144, transcendentals=0),
    )(*gradients)
    return (query_grad, key_grad, value_grad)


def solution(mesh):
    fine = Mesh(mesh.devices.reshape(4, 2, 2, 2, ZS), ("y", "xl", "c", "xh", "z"))
    tokens = P(("y", "xl", "c", "xh", "z"), None)
    in_specs = (tokens,) * 6 + (P(), P(("y", "xl", "c"), None))
    return jax.shard_map(
        shards, mesh=fine, in_specs=in_specs, out_specs=(tokens,) * 3, check_vma=False
    )
```

```python
import functools
import math

import jax
import jax.numpy as jnp
from jax import lax
from jax.experimental import pallas as pl
from jax.experimental.pallas import tpu as pltpu
from jax.sharding import Mesh
from jax.sharding import PartitionSpec as P

KVH = 8
HD = 128
GROUP = 8
BLOCK = 128
WINDOW = 2048
TOK = 32
ZS = 8
AS = 8
CHUNK = TOK * ZS
ROWS = TOK * GROUP
SCALE = 1.0 / math.sqrt(HD)
LOG2E = math.log2(math.e)
BIG = 1e30
PAIR = 2
SPAN = 4
EXTRA = 16
HEADS = ("xl", "c", "xh")
F32 = jnp.float32
BF16 = jnp.bfloat16
EARLY = (0, 1, -1)
FAR = (3, -3, 4)
LATE = (2, -2)


def along_z(value, by):
    return lax.ppermute(value, "z", [(i, (i + by) % ZS) for i in range(ZS)])


def exchange(value):
    return lax.all_to_all(value, HEADS, split_axis=0, concat_axis=0, tiled=True)


def own_place():
    return (lax.axis_index("xl") * 2 + lax.axis_index("c")) * 2 + lax.axis_index("xh")


def shifted(value, by):
    return lax.ppermute(value, HEADS, [(i, (i + by) % AS) for i in range(AS)])


def pack_kv_kernel(k_hbm, v_hbm, out_ref, k_ref, v_ref, sems):
    copies = [
        pltpu.make_async_copy(k_hbm, k_ref, sems.at[0]),
        pltpu.make_async_copy(v_hbm, v_ref, sems.at[1]),
    ]
    for copy in copies:
        copy.start()
    for n, (copy, ref) in enumerate(zip(copies, (k_ref, v_ref))):
        copy.wait()
        for a in range(AS):
            out_ref[a, :, n * HD : (n + 1) * HD] = ref[:, a * HD : (a + 1) * HD]


def split(value):
    high = value.astype(BF16)
    return high, (value - high.astype(F32)).astype(BF16)


def pack_queries_kernel(q_hbm, g_hbm, o_hbm, lse_hbm, keep_hbm, out_ref, *refs):
    q_ref, g_ref, o_ref, lse_ref, keep_ref, row_ref, sems, small = refs
    wide = GROUP * HD
    small_copies = [
        pltpu.make_async_copy(lse_hbm, lse_ref, small.at[0]),
        pltpu.make_async_copy(keep_hbm, keep_ref, small.at[1]),
    ]
    for copy in small_copies:
        copy.start()
    copies = []
    for a in range(AS):
        columns = pl.ds(a * wide, wide)
        copies.append(
            [
                pltpu.make_async_copy(src.at[:, columns], dst.at[:, columns], sems.at[n, a])
                for n, (src, dst) in enumerate(((g_hbm, g_ref), (o_hbm, o_ref), (q_hbm, q_ref)))
            ]
        )
        for copy in copies[a]:
            copy.start()
    ones = jnp.ones((8, 2 * HD), BF16)
    lane = lax.broadcasted_iota(jnp.int32, (TOK, ROWS), 1)
    spread = (lane % TOK == lax.broadcasted_iota(jnp.int32, (TOK, ROWS), 0)).astype(F32).astype(BF16)
    head_lane = lax.broadcasted_iota(jnp.int32, (GROUP, ROWS), 1) // TOK
    own_head = head_lane == lax.broadcasted_iota(jnp.int32, (GROUP, ROWS), 0)
    row = lax.broadcasted_iota(jnp.int32, (EXTRA, HD), 0)
    for copy in small_copies:
        copy.wait()
    place = lax.axis_index("xh") * 2 + lax.axis_index("z") // 4
    kept = keep_ref[...].astype(F32)
    at_place = lax.broadcasted_iota(jnp.int32, kept.shape, 0) == place
    row_ref[...] = jnp.zeros(row_ref.shape, F32)
    row_ref[0:1, : kept.shape[1]] = jnp.sum(jnp.where(at_place, kept, 0.0), axis=0, keepdims=True)
    flags = row_ref[0:1]
    scaled = lse_ref[...].T * LOG2E
    high, low = split(scaled)
    lower = split(scaled - high.astype(F32) - low.astype(F32))[0]
    lse_all = sum(jnp.dot(p, spread, preferred_element_type=F32) for p in (high, low, lower))
    for a in range(AS):
        for copy in copies[a]:
            copy.wait()
        columns = slice(a * wide, (a + 1) * wide)
        for h in range(GROUP):
            head = slice((a * GROUP + h) * HD, (a * GROUP + h + 1) * HD)
            out_ref[a, h * TOK : (h + 1) * TOK, :] = q_ref[:, head]
            out_ref[a, ROWS + h * TOK : ROWS + (h + 1) * TOK, :] = g_ref[:, head]
        product = g_ref[:, columns].astype(F32) * o_ref[:, columns].astype(F32)
        high, low = split(product)
        stacked = jnp.concatenate(
            [
                jnp.concatenate([p[:, h * HD : (h + 1) * HD] for h in range(GROUP)], axis=0)
                for p in (high, low)
            ],
            axis=1,
        )
        delta = lax.dot_general(
            ones, stacked, (((1,), (1,)), ((), ())), preferred_element_type=F32
        )[:1]
        lse = jnp.sum(
            jnp.where(own_head, lse_all[a * GROUP : (a + 1) * GROUP], 0.0), axis=0, keepdims=True
        )
        parts = [p.astype(F32) for p in split(lse) + split(delta)]
        extra = jnp.where(row == 8, flags, 0.0)
        for n, part in enumerate(parts):
            extra = jnp.where(row == 2 * n, part[:, :HD], extra)
            extra = jnp.where(row == 2 * n + 1, part[:, HD:], extra)
        out_ref[a, 2 * ROWS :, :] = extra.astype(BF16)


def attention_kernel(offsets, first_call, final, keep_ref, message_ref, start_ref, *refs):
    pieces = len(offsets)
    kv_refs, refs = refs[:pieces], refs[pieces:]
    if not first_call:
        dqt_in_ref, refs = refs[0], refs[1:]
    dq_ref, refs = refs[0], refs[1:]
    dkv_refs, refs = refs[:pieces], refs[pieces:]
    acc_ref, kt_ref, qt_ref, gt_ref, dqt_ref = refs
    z = lax.axis_index("z")
    sources = [lax.rem(z - off + ZS, ZS) for off in offsets]
    halves = [source // 4 for source in sources]
    lane_token = lax.rem(lax.broadcasted_iota(jnp.int32, (1, ROWS), 1), TOK)
    sublane = lax.broadcasted_iota(jnp.int32, (TOK, ROWS), 0)
    keys = SPAN * pieces * TOK

    def keys_of(b, lanes):
        return jnp.concatenate(
            [kv[b * SPAN + c, :, lanes] for c in range(SPAN) for kv in kv_refs], axis=0
        )

    for b in range(AS // SPAN):
        kt_ref[b] = keys_of(b, pl.ds(0, HD)).T

    def rows_of(j, first):
        return jnp.concatenate(
            [message_ref[j * PAIR + c, first : first + ROWS, :] for c in range(PAIR)], axis=0
        )

    def load(j, slot):
        vectors = []
        for c in range(PAIR):
            i = j * PAIR + c
            extra = message_ref[i, 2 * ROWS :, :].astype(F32)
            summed = [extra[n : n + 1] + extra[n + 2 : n + 3] for n in (0, 1, 4, 5)]
            lse = jnp.concatenate(summed[:2], axis=1)
            delta = jnp.concatenate(summed[2:], axis=1)
            vectors.append((lse, delta, start_ref[i], i * CHUNK + z * TOK + lane_token))
        qt_ref[slot] = rows_of(j, 0).T
        gt_ref[slot] = rows_of(j, ROWS).T
        return vectors

    def tile(j, b, slot, vectors):
        reaches_own = (b + 1) * SPAN > j * PAIR
        scores = jnp.dot(keys_of(b, pl.ds(0, HD)), qt_ref[slot], preferred_element_type=F32)
        dprobs = jnp.dot(keys_of(b, pl.ds(HD, HD)), gt_ref[slot], preferred_element_type=F32)
        probs_b, dscores_b = [], []
        for k in range(SPAN * pieces):
            a, r = b * SPAN + k // pieces, k % pieces
            rows = slice(k * TOK, (k + 1) * TOK)
            probs_row, dscores_row = [], []
            for c, (lse, delta, start, q_pos) in enumerate(vectors):
                i = j * PAIR + c
                columns = slice(c * ROWS, (c + 1) * ROWS)
                distance = 2 * (i - a) + z // 4 - halves[r]
                kept = keep_ref[i, jnp.maximum(distance, 0)] > 0
                shift = lse + jnp.where(kept, 0.0, BIG)
                probs = jnp.exp2(scores[rows, columns] * (SCALE * LOG2E) - shift)
                k_pos = a * CHUNK + sources[r] * TOK + sublane
                allowed = k_pos >= start
                if reaches_own:
                    allowed = allowed & (k_pos <= q_pos)
                probs = jnp.where(allowed, probs, 0.0)
                probs_row.append(probs.astype(BF16))
                dscores_row.append((probs * (dprobs[rows, columns] - delta)).astype(BF16))
            probs_b.append(jnp.concatenate(probs_row, axis=1))
            dscores_b.append(jnp.concatenate(dscores_row, axis=1))
        probs_b = jnp.concatenate(probs_b, axis=0)
        dscores_b = jnp.concatenate(dscores_b, axis=0)
        dk = jnp.dot(dscores_b, rows_of(j, 0), preferred_element_type=F32)
        dv = jnp.dot(probs_b, rows_of(j, ROWS), preferred_element_type=F32)
        if j == b * SPAN // PAIR:
            acc_ref[b, :, :HD] = dk
            acc_ref[b, :, HD:] = dv
        else:
            acc_ref[b, :, :HD] += dk
            acc_ref[b, :, HD:] += dv
        dq = jnp.dot(kt_ref[b], dscores_b, preferred_element_type=F32)
        if b == 0 and first_call:
            dqt_ref[slot] = dq
        elif b == 0:
            dqt_ref[slot] = dqt_in_ref[j] + dq
        else:
            dqt_ref[slot] += dq

    for j in range(AS // PAIR):
        slot = j % 2
        vectors = load(j, slot)
        for b in range(j * PAIR // SPAN + 1):
            tile(j, b, slot, vectors)
        if not final:
            dq_ref[j] = dqt_ref[slot]
            continue
        dq = (dqt_ref[slot] * SCALE).T.astype(BF16)
        for c in range(PAIR):
            for h in range(GROUP):
                at = c * ROWS + h * TOK
                dq_ref[j * PAIR + c, :, h * HD : (h + 1) * HD] = dq[at : at + TOK]

    for b in range(AS // SPAN):
        for k in range(SPAN * pieces):
            piece = acc_ref[b, k * TOK : (k + 1) * TOK, :]
            out = dkv_refs[k % pieces].at[b * SPAN + k // pieces]
            out[:, :HD] = (piece[:, :HD] * SCALE).astype(BF16)
            out[:, HD:] = piece[:, HD:].astype(BF16)


def attention(offsets, keep, message, start, kv, dqt=None, final=False):
    first_call = dqt is None
    pieces = len(offsets)
    keys = SPAN * pieces * TOK
    rows = PAIR * ROWS
    dqt_shape = jax.ShapeDtypeStruct((AS // PAIR, HD, rows), F32)
    dq_shape = jax.ShapeDtypeStruct((AS, TOK, GROUP * HD), BF16)
    results = pl.pallas_call(
        functools.partial(attention_kernel, offsets, first_call, final),
        out_shape=[dq_shape if final else dqt_shape]
        + [jax.ShapeDtypeStruct((AS, TOK, 2 * HD), BF16)] * pieces,
        in_specs=[in_smem()] + [in_vmem()] * (2 + pieces + (not first_call)),
        out_specs=[in_vmem()] * (1 + pieces),
        scratch_shapes=[
            pltpu.VMEM((AS // SPAN, keys, 2 * HD), F32),
            pltpu.VMEM((AS // SPAN, HD, keys), BF16),
            pltpu.VMEM((2, HD, rows), BF16),
            pltpu.VMEM((2, HD, rows), BF16),
            pltpu.VMEM((2, HD, rows), F32),
        ],
        compiler_params=pltpu.CompilerParams(vmem_limit_bytes=24 * 2**20),
        cost_estimate=pl.CostEstimate(
            flops=400000000 * pieces, bytes_accessed=3000000, transcendentals=300000 * pieces
        ),
    )(keep, message, start, *[kv[o] for o in offsets], *([] if first_call else [dqt]))
    return results[0], dict(zip(offsets, results[1:]))


def sum_kernel(*refs):
    total = refs[0][...].astype(F32)
    for ref in refs[1:-1]:
        total = total + ref[...].astype(F32)
    refs[-1][...] = total.astype(BF16)


def pack_gradients_kernel(*refs):
    pieces, out_refs, (total_ref,) = refs[:5], refs[5 : 5 + AS], refs[5 + AS :]
    me = own_place()
    total = pieces[0][...].astype(F32)
    for piece in pieces[1:]:
        total = total + piece[...].astype(F32)
    total_ref[...] = total.astype(BF16)
    for k, out_ref in enumerate(out_refs):
        there = lax.rem(me + k, AS)
        for n in range(TOK // 8):
            columns = slice(n * 2 * HD, (n + 1) * 2 * HD)
            out_ref[:, columns] = total_ref[there, n * 8 : (n + 1) * 8, :]


def unpack_queries_kernel(in_ref, out_hbm, sems):
    wide = GROUP * HD
    copies = [
        pltpu.make_async_copy(in_ref.at[a], out_hbm.at[:, pl.ds(a * wide, wide)], sems.at[a])
        for a in range(AS)
    ]
    for copy in copies:
        copy.start()
    for copy in copies:
        copy.wait()


def unpack_gradients_kernel(*refs):
    in_refs, (dk_ref, dv_ref) = refs[:AS], refs[AS:]
    me = own_place()
    for k, in_ref in enumerate(in_refs):
        a = lax.rem(me - k + AS, AS)
        columns = pl.ds(pl.multiple_of(a * HD, HD), HD)
        for n in range(TOK // 8):
            rows = slice(n * 8, (n + 1) * 8)
            dk_ref[rows, columns] = in_ref[:, 2 * n * HD : (2 * n + 1) * HD]
            dv_ref[rows, columns] = in_ref[:, (2 * n + 1) * HD : (2 * n + 2) * HD]


def in_hbm():
    return pl.BlockSpec(memory_space=pltpu.HBM)


def held_in_hbm(*values):
    return [pltpu.with_memory_space_constraint(v, pltpu.HBM) for v in values]


def anywhere():
    return pl.BlockSpec(memory_space=pl.ANY)


def in_vmem():
    return pl.BlockSpec(memory_space=pltpu.VMEM)


def in_smem():
    return pl.BlockSpec(memory_space=pltpu.SMEM)


def partial_sum(*values):
    shape = values[0].shape
    return pl.pallas_call(
        sum_kernel,
        out_shape=jax.ShapeDtypeStruct(shape, BF16),
        in_specs=[in_vmem()] * len(values),
        out_specs=in_vmem(),
        compiler_params=pltpu.CompilerParams(vmem_limit_bytes=4 * 2**20),
        cost_estimate=pl.CostEstimate(
            flops=65536 * len(values), bytes_accessed=131072 * (1 + len(values)), transcendentals=0
        ),
    )(*values)


def shards(query, key, value, output, out_grad, lse, doc_lengths, block_keep):
    i32 = jnp.int32
    z = lax.axis_index("z").astype(i32)
    columns = GROUP * HD
    dma = pltpu.SemaphoreType.DMA
    small_kernel = pltpu.CompilerParams(vmem_limit_bytes=4 * 2**20)

    kv_send = pl.pallas_call(
        pack_kv_kernel,
        out_shape=jax.ShapeDtypeStruct((AS, TOK, 2 * HD), BF16),
        in_specs=[in_hbm(), in_hbm()],
        out_specs=in_vmem(),
        scratch_shapes=[pltpu.VMEM(key.shape, BF16), pltpu.VMEM(key.shape, BF16), dma((2,))],
        compiler_params=small_kernel,
        cost_estimate=pl.CostEstimate(flops=0, bytes_accessed=262144, transcendentals=0),
    )(*held_in_hbm(key, value))
    kv_own = exchange(kv_send)

    reach = block_keep.shape[1]
    message_send = pl.pallas_call(
        pack_queries_kernel,
        out_shape=jax.ShapeDtypeStruct((AS, 2 * ROWS + EXTRA, HD), BF16),
        in_specs=[in_hbm()] * 5,
        out_specs=in_vmem(),
        scratch_shapes=[
            pltpu.VMEM((TOK, AS * columns), BF16),
            pltpu.VMEM((TOK, AS * columns), BF16),
            pltpu.VMEM((TOK, AS * columns), BF16),
            pltpu.VMEM(lse.shape, F32),
            pltpu.VMEM(block_keep.shape, i32),
            pltpu.VMEM((8, HD), F32),
            dma((3, AS)),
            dma((2,)),
        ],
        compiler_params=pltpu.CompilerParams(vmem_limit_bytes=8 * 2**20),
        cost_estimate=pl.CostEstimate(flops=67108864, bytes_accessed=2800000, transcendentals=0),
    )(*held_in_hbm(query, out_grad, output, lse, block_keep))
    message = exchange(message_send)

    pieces = {0: kv_own}
    for off in (1, -1, 2, -2):
        pieces[off] = along_z(kv_own, off)
    pieces[3] = along_z(pieces[2], 1)
    pieces[-3] = along_z(pieces[-2], -1)
    pieces[4] = along_z(pieces[2], 2)

    keep = message[:, 2 * ROWS + 8, :reach].astype(i32)
    ends = jnp.arange(doc_lengths.shape[0], dtype=i32)
    starts = jnp.sum(jnp.where(ends[None, :] < ends[:, None], doc_lengths[None, :], 0), axis=1)
    base = lax.axis_index("y").astype(i32) * WINDOW
    positions = (
        base
        + jnp.arange(AS, dtype=i32)[:, None] * CHUNK
        + z * TOK
        + (jnp.arange(ROWS, dtype=i32) % TOK)[None, :]
    )
    start_of = jnp.max(
        jnp.where(starts[None, None, :] <= positions[:, :, None], starts[None, None, :], 0), axis=2
    )
    start_of = jnp.maximum(start_of - base, 0)

    start = start_of.reshape(AS, 1, ROWS)
    dqt, part = attention(EARLY, keep, message, start, pieces)
    one, minus_one = along_z(part[1], -1), along_z(part[-1], 1)
    dqt, far_part = attention(FAR, keep, message, start, pieces, dqt)
    from_three, from_four = along_z(far_part[3], -1), along_z(far_part[4], -2)
    from_minus_three = along_z(far_part[-3], 1)
    dqt, one, minus_one = lax.optimization_barrier((dqt, one, minus_one))
    dq, late_part = attention(LATE, keep, message, start, pieces, dqt, final=True)
    two = along_z(partial_sum(late_part[2], from_three, from_four), -2)
    minus_two = along_z(partial_sum(late_part[-2], from_minus_three), 2)
    dq_back = exchange(dq)
    returned = (part[0], one, minus_one, two, minus_two)
    query_grad = pl.pallas_call(
        unpack_queries_kernel,
        out_shape=jax.ShapeDtypeStruct((TOK, AS * columns), BF16),
        in_specs=[in_vmem()],
        out_specs=in_hbm(),
        scratch_shapes=[dma((AS,))],
        compiler_params=small_kernel,
        cost_estimate=pl.CostEstimate(flops=0, bytes_accessed=1048576, transcendentals=0),
    )(dq_back)
    gradients = pl.pallas_call(
        pack_gradients_kernel,
        out_shape=[jax.ShapeDtypeStruct((8, columns), BF16)] * AS,
        in_specs=[in_vmem()] * 5,
        out_specs=[in_vmem()] * AS,
        scratch_shapes=[pltpu.VMEM((AS, TOK, 2 * HD), BF16)],
        compiler_params=small_kernel,
        cost_estimate=pl.CostEstimate(flops=5000000000, bytes_accessed=900000, transcendentals=0),
    )(*returned)
    gradients = [gradients[0]] + [shifted(gradients[k], k) for k in range(1, AS)]
    query_grad, gradients = lax.optimization_barrier((query_grad, gradients))
    half = jax.ShapeDtypeStruct((TOK, KVH * HD), BF16)
    key_grad, value_grad = pl.pallas_call(
        unpack_gradients_kernel,
        out_shape=[half, half],
        in_specs=[in_vmem()] * AS,
        out_specs=[in_vmem()] * 2,
        compiler_params=small_kernel,
        cost_estimate=pl.CostEstimate(flops=0, bytes_accessed=262144, transcendentals=0),
    )(*gradients)
    return (query_grad, key_grad, value_grad)


def solution(mesh):
    fine = Mesh(mesh.devices.reshape(4, 2, 2, 2, ZS), ("y", "xl", "c", "xh", "z"))
    tokens = P(("y", "xl", "c", "xh", "z"), None)
    in_specs = (tokens,) * 6 + (P(), P(("y", "xl", "c"), None))
    return jax.shard_map(
        shards, mesh=fine, in_specs=in_specs, out_specs=(tokens,) * 3, check_vma=False
    )
```
